512 devices in a mesh: seq: 64 (over x_hi, z, core), head: 8 (over x_lo, y).
Axes of the slice: x: 4 (x_hi: 2, x_lo: 2; x = x_hi * 2 + x_lo), y: 4, z: 16, core: 2. Of those that a mesh axis runs over, the one named last changes fastest.
Arguments:
- queries: bfloat16 [24576, 8192], P(('seq', 'head')), may hold values from -26 to 26
- keys: bfloat16 [24576, 1024], P(('seq', 'head')), may hold values from -6 to 6
- values: bfloat16 [24576, 1024], P(('seq', 'head')), may hold values from -6 to 6
- block_list: int32 [8, 192, 32], replicated, may hold values from 0 to 191, as said below
- block_count: int32 [8, 192], replicated, may hold values from 1 to 32
Outputs:
- attended: bfloat16 [24576, 8192], P(('seq', 'head'))
The draws below stay inside these ranges and needn't reach their ends.
Inputs may be any that keep to these rules, and one draw needn't show every extreme that they name: `block_list`: for each key-value head and query block b, the used entries are distinct key blocks, none after b, and unused entries are 0. For each key-value head, the query blocks of one sequence shard (3 blocks) together list at most one block of each other shard, from at most 29 other shards.
All inputs are finite; a program needn't handle non-finite values.
Results may differ from the reference program's by a relative error of at most 0.0045.
Values may be sent and summed in bfloat16 or wider, within the bound.
A program may use at most 64 MiB of HBM per device.

```python
import math
import jax
import jax.numpy as jnp
from jax import lax

HEADS = 64
KV_HEADS = 8
HEAD_DIM = 128
BLOCK = 128
STEP = 8
TOK_DEV = 384
SHARDS = 64
TOKENS = 24576
BLOCKS = 192
R_HEAVY = 29
R_LIGHT = 9
MAXSEL = 32


def shuffle_one(subkey):
    return jax.random.permutation(subkey, SHARDS)


def block_pattern(key):
    seeded = jax.random.fold_in(key, 41)
    subkeys = jax.random.split(seeded, 4)
    per_shard = TOK_DEV // BLOCK
    shard_ids = jnp.arange(SHARDS, dtype=jnp.int32)
    shuffled = jax.vmap(shuffle_one)(jax.random.split(subkeys[0], KV_HEADS))
    forced = jax.random.randint(subkeys[1], (KV_HEADS,), R_HEAVY, SHARDS)
    crowded = (shuffled < SHARDS // 4) | (shard_ids[None, :] == forced[:, None])
    remote = jnp.where(crowded, jnp.minimum(shard_ids, R_HEAVY), jnp.minimum(shard_ids, R_LIGHT))
    priority = jax.vmap(shuffle_one)(jax.random.split(subkeys[2], KV_HEADS * SHARDS))
    priority = priority.reshape(KV_HEADS, SHARDS, SHARDS)
    owner_ids = shard_ids[None, None, :]
    reader_ids = shard_ids[None, :, None]
    forced_owner = (owner_ids == reader_ids - 1) | (owner_ids == 0)
    ranking_key = jnp.where(owner_ids < reader_ids, priority + jnp.where(forced_owner, SHARDS, 0), -1 - owner_ids)
    ordering = jnp.argsort(-ranking_key, axis=-1)
    position_rank = jnp.argsort(ordering, axis=-1)
    chosen = position_rank < remote[:, :, None]
    block_pick = jax.random.randint(subkeys[3], (KV_HEADS, SHARDS, SHARDS), 0, per_shard)
    block_pick = jnp.where(owner_ids == reader_ids - 1, per_shard - 1, jnp.where(owner_ids == 0, 0, block_pick))
    global_block = owner_ids * per_shard + block_pick
    sort_key = jnp.where(chosen, owner_ids, SHARDS + owner_ids)
    listing = jnp.take_along_axis(global_block, jnp.argsort(sort_key, axis=-1), axis=-1)[:, :, :R_HEAVY]
    padded_remote = jnp.concatenate([listing, jnp.zeros((KV_HEADS, SHARDS, per_shard), jnp.int32)], axis=-1)
    slot_ids = jnp.arange(MAXSEL, dtype=jnp.int32)[None, None, None, :]
    local_ids = jnp.arange(per_shard, dtype=jnp.int32)[None, None, :, None]
    reach = remote[:, :, None, None]
    own_block = shard_ids[None, :, None, None] * per_shard + slot_ids - reach
    entries = jnp.where(slot_ids < reach, padded_remote[:, :, None, :], jnp.where(slot_ids < reach + local_ids + 1, own_block, 0))
    counts = remote[:, :, None] + jnp.arange(per_shard, dtype=jnp.int32)[None, None, :] + 1
    return (entries.reshape(KV_HEADS, SHARDS * per_shard, MAXSEL).astype(jnp.int32), counts.reshape(KV_HEADS, SHARDS * per_shard).astype(jnp.int32))


def query_key_fields(key):
    seeded = jax.random.fold_in(key, 23)
    draw_one, draw_two = jax.random.split(seeded, 2)
    query = jax.random.truncated_normal(draw_one, -6.0, 6.0, (TOKENS, HEADS * HEAD_DIM), jnp.float32)
    keyed = jax.random.truncated_normal(draw_two, -6.0, 6.0, (TOKENS, KV_HEADS * HEAD_DIM), jnp.float32)
    return (query, keyed)


def draw_queries(key, part):
    return query_key_fields(key)[0].astype(jnp.bfloat16)


def draw_keys(key, part):
    return query_key_fields(key)[1].astype(jnp.bfloat16)


def draw_block_list(key, part):
    return block_pattern(key)[0]


def draw_block_count(key, part):
    return block_pattern(key)[1]


def levels(key, shape, cuts, low, top_value):
    factor_of = 1.0
    for dim, parts in cuts:
        heights = jax.random.uniform(jax.random.fold_in(jax.random.fold_in(key, 6), dim), (parts,), jnp.float32, low / len(cuts), top_value / len(cuts))
        factor_of = factor_of * jnp.repeat(jnp.exp(heights), shape[dim] // parts).reshape((-1,) + (1,) * (len(shape) - 1 - dim))
    return factor_of


def gaussian(key, shape, width, bound, pieces=(), held_as=jnp.bfloat16):
    values = width * jax.random.normal(key, shape, jnp.float32)
    if pieces:
        values = values * levels(key, shape, pieces, -0.22, 0.18)
    return jnp.clip(values, -bound, bound).astype(held_as)


def setup_inputs(seed: int = 0) -> dict:
    seeds = jax.random.split(jax.random.key(seed), 6)
    queries = draw_queries(jax.random.fold_in(seeds[5], 71), 0)
    keys = draw_keys(jax.random.fold_in(seeds[5], 71), 0)
    values = gaussian(seeds[2], (TOKENS, KV_HEADS * HEAD_DIM), 1.0, 6.0, ((0, 512),))
    block_list = draw_block_list(jax.random.fold_in(seeds[5], 71), 0)
    block_count = draw_block_count(jax.random.fold_in(seeds[5], 71), 0)
    return {"queries": queries, "keys": keys, "values": values, "block_list": block_list, "block_count": block_count}


def attend(block_q, key_group, value_group, entries, listed_count, block_index):
    per_kv = HEADS // KV_HEADS
    inverse_root = 1.0 / math.sqrt(HEAD_DIM)
    query_f = block_q.astype(jnp.float32)
    offsets = jnp.arange(BLOCK, dtype=jnp.int32)
    query_position = block_index * BLOCK + offsets
    running = jnp.full((per_kv, BLOCK), -1e+30, jnp.float32)
    denominator = jnp.zeros((per_kv, BLOCK), jnp.float32)
    accumulated = jnp.zeros((per_kv, BLOCK, HEAD_DIM), jnp.float32)
    for step_index in range(entries.shape[0] // STEP):
        selected = entries[step_index * STEP:(step_index + 1) * STEP]
        key_rows = key_group[selected].reshape(STEP * BLOCK, HEAD_DIM).astype(jnp.float32)
        value_rows = value_group[selected].reshape(STEP * BLOCK, HEAD_DIM).astype(jnp.float32)
        key_position = (selected[:, None] * BLOCK + offsets[None, :]).reshape(-1)
        usable = jnp.repeat(step_index * STEP + jnp.arange(STEP, dtype=jnp.int32) < listed_count, BLOCK)
        allowed = usable[None, :] & (key_position[None, :] <= query_position[:, None])
        scores = jnp.einsum('qhd,kd->hqk', query_f, key_rows) * inverse_root
        scores = jnp.where(allowed[None, :, :], scores, jnp.float32(-1e+30))
        newest = jnp.maximum(running, lax.optimization_barrier(jnp.max(scores, axis=-1)))
        rescale = jnp.exp(running - newest)
        prob = jnp.exp(scores - newest[..., None])
        denominator = denominator * rescale + lax.optimization_barrier(jnp.sum(prob, axis=-1))
        weights = lax.optimization_barrier(prob.astype(jnp.bfloat16)).astype(jnp.float32)
        accumulated = accumulated * rescale[..., None] + jnp.einsum('hqk,kd->hqd', weights, value_rows)
        running = newest
    result = accumulated / denominator[..., None]
    return result.transpose(1, 0, 2).reshape(BLOCK, per_kv * HEAD_DIM).astype(jnp.bfloat16)

def reference(queries, keys, values, block_list, block_count):
    per_kv = HEADS // KV_HEADS
    padded_width = (MAXSEL + STEP - 1) // STEP * STEP
    padded_lists = jnp.pad(block_list, ((0, 0), (0, 0), (0, padded_width - MAXSEL)))
    query_all = queries.reshape(BLOCKS, BLOCK, KV_HEADS, per_kv, HEAD_DIM)
    key_all = keys.reshape(BLOCKS, BLOCK, KV_HEADS, HEAD_DIM)
    value_all = values.reshape(BLOCKS, BLOCK, KV_HEADS, HEAD_DIM)

    def per_group(kv_group):
        key_group = key_all[:, :, kv_group]
        value_group = value_all[:, :, kv_group]

        def per_block(block_index):
            block_q = query_all[block_index][:, kv_group]
            return attend(block_q, key_group, value_group, padded_lists[kv_group, block_index], block_count[kv_group, block_index], block_index)
        return lax.map(per_block, jnp.arange(BLOCKS, dtype=jnp.int32))
    outputs = lax.map(per_group, jnp.arange(KV_HEADS, dtype=jnp.int32))
    return outputs.transpose(1, 2, 0, 3).reshape(TOKENS, HEADS * HEAD_DIM)
```

```python
import functools
import math

import jax
import jax.numpy as jnp
from jax import lax
from jax.experimental import pallas as pl
from jax.experimental.pallas import tpu as pltpu
from jax.sharding import PartitionSpec as P

HEADS = 64
KV_HEADS = 8
HEAD_DIM = 128
BLOCK = 128
GROUP = 4
RINGED = 3
CORES = 2
HALVES = 2
MESH = pl.DeviceIdType.MESH
OWN, RING, EARLY, CROSS, MATE, MATE_EARLY, MATE_CROSS = range(7)


def gather_kernel(
    shards, heads, q_ref, k_ref, v_ref, qo_ref, tab_ref, kv_send, kv_recv, q_send, q_recv, send, recv, local
):
    rows = k_ref.shape[0]
    per_shard = tab_ref.shape[2]
    q_cols = q_ref.shape[1] // heads
    depth = shards // (CORES * HALVES)
    far = depth // 2
    early_rows = RINGED * per_shard // 3
    s = lax.axis_index("seq")
    h = lax.axis_index("head")
    core = s % CORES
    z = (s // CORES) % depth
    half = s // (CORES * depth)

    def seq_at(half_at, z_at):
        return (half_at * depth + z_at) * CORES + core

    up = seq_at(half, (z + 1) % depth)
    down = seq_at(half, (z + depth - 1) % depth)
    mate = s + 1 - 2 * core
    across = seq_at(1 - half, z)
    here = pl.ds(pl.multiple_of(h * rows, 16), rows)

    barrier = pltpu.get_barrier_semaphore()
    for d in range(1, heads):
        pl.semaphore_signal(barrier, inc=1, device_id=(s, (h + d) % heads), device_id_type=MESH)
    for other in (up, down, mate, across):
        pl.semaphore_signal(barrier, inc=1, device_id=(other, h), device_id_type=MESH)
    pl.semaphore_wait(barrier, heads + 3)

    def remote(src, dst, send_sem, recv_sem, to):
        return pltpu.make_async_remote_copy(
            src_ref=src, dst_ref=dst, send_sem=send_sem, recv_sem=recv_sem, device_id=to, device_id_type=MESH
        )

    kv_copies, q_copies = [], []
    for d in range(1, heads):
        peer = (h + d) % heads
        cols = pl.ds(pl.multiple_of(peer * HEAD_DIM, HEAD_DIM), HEAD_DIM)
        for i, ref in enumerate((k_ref, v_ref)):
            kv_copies.append(
                remote(ref.at[:, cols], tab_ref.at[s, i, here], kv_send.at[i, d], kv_recv.at[i, d], (s, peer))
            )
        wide = pl.ds(pl.multiple_of(peer * q_cols, HEAD_DIM), q_cols)
        q_copies.append(remote(q_ref.at[:, wide], qo_ref.at[here], q_send.at[d], q_recv.at[d], (s, peer)))
    cols = pl.ds(pl.multiple_of(h * HEAD_DIM, HEAD_DIM), HEAD_DIM)
    wide = pl.ds(pl.multiple_of(h * q_cols, HEAD_DIM), q_cols)
    kv_local = [
        pltpu.make_async_copy(ref.at[:, cols], tab_ref.at[s, i, here], local.at[i])
        for i, ref in enumerate((k_ref, v_ref))
    ]
    q_local = pltpu.make_async_copy(q_ref.at[:, wide], qo_ref.at[here], local.at[2])
    for copy in kv_copies + kv_local:
        copy.start()
    for copy in kv_local:
        copy.wait()
    for copy in kv_copies:
        copy.wait_recv()

    def flow(mine):
        sent = []

        def chunk(half_at, way, t):
            z_at = (z - t + depth) % depth if way == 0 else (z + t) % depth
            return seq_at(half_at, z_at)

        def piece(kind, way, t):
            late = per_shard - early_rows
            if kind in (RING, MATE):
                at = chunk(mine, way, t)
                return tab_ref.at[at, way] if t == far else tab_ref.at[at]
            at = chunk(0, way, t)
            span = pl.ds(0, early_rows) if kind in (EARLY, MATE_EARLY, OWN) else pl.ds(early_rows, late)
            return tab_ref.at[at, way, span] if t == far else tab_ref.at[at, :, span]

        def copy_of(kind, way, t):
            to = {RING: (up, down)[way], EARLY: (up, down)[way], OWN: across, CROSS: across}.get(kind, mate)
            slot = t + 1 if kind in (RING, EARLY) else t
            if slot == far and kind in (RING, EARLY):
                at = chunk(mine if kind == RING else 0, way, t)
                ref = tab_ref.at[at, way] if kind == RING else tab_ref.at[at, way, pl.ds(0, early_rows)]
            else:
                ref = piece(kind, way, t)
            return remote(ref, ref, send.at[kind, way, slot], recv.at[kind, way, slot], (to, h))

        def go(kind, way, t):
            copy = copy_of(kind, way, t)
            copy.start()
            sent.append(copy)

        def arrive(kind, way, slot):
            if kind in (RING, EARLY):
                half_at = mine if kind == RING else 0
                at = chunk(half_at, way, slot)
                if kind == RING:
                    ref = tab_ref.at[at, way] if slot == far else tab_ref.at[at]
                else:
                    span = pl.ds(0, early_rows)
                    ref = tab_ref.at[at, way, span] if slot == far else tab_ref.at[at, :, span]
                to = (up, down)[way]
            elif kind in (MATE, MATE_EARLY, MATE_CROSS):
                z_at = (z - slot + depth) % depth if way == 0 else (z + slot) % depth
                at = (((mine if kind == MATE else 0) * depth + z_at) * CORES) + 1 - core
                span = pl.ds(0, early_rows) if kind == MATE_EARLY else pl.ds(early_rows, per_shard - early_rows)
                if kind == MATE:
                    ref = tab_ref.at[at, way] if slot == far else tab_ref.at[at]
                else:
                    ref = tab_ref.at[at, way, span] if slot == far else tab_ref.at[at, :, span]
                to = mate
            else:
                ref = piece(kind, way, slot)
                to = across
            remote(ref, ref, send.at[kind, way, slot], recv.at[kind, way, slot], (to, h)).wait_recv()

        crossing = early_rows < per_shard
        stages = [(0, 0)] + [(t, way) for t in range(1, far + 1) for way in (0, 1)]
        for way in (0, 1):
            go(RING, way, 0)
        if mine == 0:
            go(OWN, 0, 0)
        go(MATE, 0, 0)
        if mine == 0 and crossing:
            go(CROSS, 0, 0)
        for copy in q_copies + [q_local]:
            copy.start()
        if mine == 1:
            arrive(OWN, 0, 0)
            for way in (0, 1):
                go(EARLY, way, 0)
            go(MATE_EARLY, 0, 0)
        pending = [(0, 0)]
        for t in range(1, far + 1):
            for way in (0, 1):
                arrive(RING, way, t)
                if t < far:
                    go(RING, way, t)
                go(MATE, way, t)
                if mine == 0 and crossing:
                    go(CROSS, way, t)
            if mine == 1:
                for way in (0, 1):
                    arrive(EARLY, way, t)
                    if t < far:
                        go(EARLY, way, t)
                    go(MATE_EARLY, way, t)
                if crossing:
                    while pending and pending[0][0] < t - 1:
                        at_t, at_way = pending.pop(0)
                        arrive(CROSS, at_way, at_t)
                        go(MATE_CROSS, at_way, at_t)
                    pending += [(t, 0), (t, 1)]
        if mine == 1 and crossing:
            for at_t, at_way in pending:
                arrive(CROSS, at_way, at_t)
                go(MATE_CROSS, at_way, at_t)
        for t, way in stages:
            arrive(MATE, way, t)
            if mine == 1:
                arrive(MATE_EARLY, way, t)
                if crossing:
                    arrive(MATE_CROSS, way, t)
        for copy in sent:
            copy.wait_send()

    @pl.when(half == 0)
    def _():
        flow(0)

    @pl.when(half == 1)
    def _():
        flow(1)

    for copy in kv_copies:
        copy.wait_send()
    q_local.wait()
    for copy in q_copies:
        copy.wait()


def gather(queries, keys, values, shards, heads):
    rows = queries.shape[0]
    depth = shards // (CORES * HALVES)
    far = depth // 2
    anywhere = pl.BlockSpec(memory_space=pl.ANY)
    dma = pltpu.SemaphoreType.DMA
    return pl.pallas_call(
        functools.partial(gather_kernel, shards, heads),
        out_shape=(
            jax.ShapeDtypeStruct((rows * heads, queries.shape[1] // heads), jnp.bfloat16),
            jax.ShapeDtypeStruct((shards, 2, rows * heads, HEAD_DIM), jnp.bfloat16),
        ),
        in_specs=[anywhere] * 3,
        out_specs=(anywhere, anywhere),
        scratch_shapes=[
            dma((2, heads)),
            dma((2, heads)),
            dma((heads,)),
            dma((heads,)),
            dma((7, 2, far + 1)),
            dma((7, 2, far + 1)),
            dma((3,)),
        ],
        compiler_params=pltpu.CompilerParams(collective_id=0, has_side_effects=True),
    )(queries, keys, values)


def attend_kernel(list_ref, count_ref, q_ref, tab_ref, o_ref, kv_ref, m_ref, acc_ref, sems):
    blocks = q_ref.shape[0] // BLOCK
    per_kv = q_ref.shape[1] // HEAD_DIM
    width = list_ref.shape[1]
    scale = math.log2(math.e) / math.sqrt(HEAD_DIM)
    first = lax.axis_index("seq") * blocks

    def groups_of(b):
        return (count_ref[b] + GROUP - 1) // GROUP

    def block_copy(b, j):
        entry = jnp.where(j < count_ref[b], list_ref[b, j], first)
        rows = pl.ds(pl.multiple_of((entry % blocks) * BLOCK, BLOCK), BLOCK)
        return pltpu.make_async_copy(tab_ref.at[entry // blocks, :, rows], kv_ref.at[b, j], sems.at[b, j])

    for b in range(blocks):

        @pl.loop(0, groups_of(b) * GROUP)
        def _(j):
            block_copy(b, j).start()

    @pl.loop(0, blocks)
    def _(b):
        m_ref[...] = jnp.full(m_ref.shape, -1e30, jnp.float32)
        acc_ref[...] = jnp.zeros(acc_ref.shape, jnp.float32)
        query_rows = pl.ds(pl.multiple_of(b * BLOCK, BLOCK), BLOCK)
        count = count_ref[b]

        def update(g, masked):
            k = kv_ref[b, pl.ds(g * GROUP, GROUP), 0].reshape(GROUP * BLOCK, HEAD_DIM)
            v = kv_ref[b, pl.ds(g * GROUP, GROUP), 1].reshape(GROUP * BLOCK, HEAD_DIM)
            v = jnp.concatenate([v, jnp.ones_like(v)], axis=1)
            if masked:
                row = lax.broadcasted_iota(jnp.int32, (BLOCK, BLOCK), 0)
                col = lax.broadcasted_iota(jnp.int32, (BLOCK, BLOCK), 1)
                limits = []
                for i in range(GROUP):
                    j = g * GROUP + i
                    own = list_ref[b, j] == first + b
                    limit = jnp.where(own, row, jnp.full_like(row, BLOCK))
                    limits.append(jnp.where(j < count, limit, jnp.full_like(row, -1)) >= col)
                allowed = jnp.concatenate([limit.astype(jnp.int32) for limit in limits], axis=1) > 0
            for head in range(per_kv):
                q = q_ref[query_rows, pl.ds(head * HEAD_DIM, HEAD_DIM)]
                scores = lax.dot_general(
                    q, k, (((1,), (1,)), ((), ())), preferred_element_type=jnp.float32
                )
                if masked:
                    scores = jnp.where(allowed, scores, jnp.float32(-1e30))
                before = m_ref[head][:, :1]
                newest = jnp.maximum(before, jnp.max(scores, axis=1, keepdims=True))
                prob = jnp.exp2(scores * scale - newest * scale)
                rescale = jnp.exp2(before * scale - newest * scale)
                acc_ref[head] = acc_ref[head] * rescale + jnp.dot(
                    prob.astype(jnp.bfloat16), v, preferred_element_type=jnp.float32
                )
                m_ref[head] = jnp.broadcast_to(newest, (BLOCK, BLOCK))

        @pl.loop(0, groups_of(b))
        def _(g):
            masked = (g + 1) * GROUP > count
            for i in range(GROUP):
                j = g * GROUP + i
                block_copy(b, j).wait()
                masked = masked | (list_ref[b, j] == first + b)

            @pl.when(masked)
            def _():
                update(g, True)

            @pl.when(jnp.logical_not(masked))
            def _():
                update(g, False)

        for head in range(per_kv):
            acc = acc_ref[head]
            o_ref[query_rows, pl.ds(head * HEAD_DIM, HEAD_DIM)] = (
                acc[:, :HEAD_DIM] / acc[:, HEAD_DIM:]
            ).astype(jnp.bfloat16)


def attend(entries, counts, queries, table):
    blocks = queries.shape[0] // BLOCK
    per_kv = queries.shape[1] // HEAD_DIM
    width = entries.shape[1]
    whole = pl.BlockSpec(memory_space=pltpu.VMEM)
    scalars = pl.BlockSpec(memory_space=pltpu.SMEM)
    return pl.pallas_call(
        attend_kernel,
        out_shape=jax.ShapeDtypeStruct(queries.shape, jnp.bfloat16),
        in_specs=[scalars, scalars, whole, pl.BlockSpec(memory_space=pl.ANY)],
        out_specs=whole,
        scratch_shapes=[
            pltpu.VMEM((blocks, width, 2, BLOCK, HEAD_DIM), jnp.bfloat16),
            pltpu.VMEM((per_kv, BLOCK, BLOCK), jnp.float32),
            pltpu.VMEM((per_kv, BLOCK, 2 * HEAD_DIM), jnp.float32),
            pltpu.SemaphoreType.DMA((blocks, width)),
        ],
        compiler_params=pltpu.CompilerParams(vmem_limit_bytes=40 * 1024 * 1024),
    )(entries, counts, queries, table)


def return_kernel(heads, o_ref, out_ref, send, recv, local):
    rows = out_ref.shape[0]
    cols = o_ref.shape[1]
    s = lax.axis_index("seq")
    h = lax.axis_index("head")
    barrier = pltpu.get_barrier_semaphore()
    for d in range(1, heads):
        pl.semaphore_signal(barrier, inc=1, device_id=(s, (h + d) % heads), device_id_type=MESH)
    pl.semaphore_wait(barrier, heads - 1)
    mine = pl.ds(pl.multiple_of(h * cols, HEAD_DIM), cols)
    copies = []
    for d in range(1, heads):
        peer = (h + d) % heads
        copies.append(
            pltpu.make_async_remote_copy(
                src_ref=o_ref.at[pl.ds(pl.multiple_of(peer * rows, 16), rows)],
                dst_ref=out_ref.at[:, mine],
                send_sem=send.at[d],
                recv_sem=recv.at[d],
                device_id=(s, peer),
                device_id_type=MESH,
            )
        )
    own = pltpu.make_async_copy(
        o_ref.at[pl.ds(pl.multiple_of(h * rows, 16), rows)], out_ref.at[:, mine], local
    )
    for copy in copies + [own]:
        copy.start()
    for copy in copies + [own]:
        copy.wait()


def give_back(attended, heads):
    rows, cols = attended.shape
    anywhere = pl.BlockSpec(memory_space=pl.ANY)
    return pl.pallas_call(
        functools.partial(return_kernel, heads),
        out_shape=jax.ShapeDtypeStruct((rows // heads, cols * heads), jnp.bfloat16),
        in_specs=[anywhere],
        out_specs=anywhere,
        scratch_shapes=[
            pltpu.SemaphoreType.DMA((heads,)),
            pltpu.SemaphoreType.DMA((heads,)),
            pltpu.SemaphoreType.DMA,
        ],
        compiler_params=pltpu.CompilerParams(collective_id=1, has_side_effects=True),
    )(attended)


def per_device(queries, keys, values, block_list, block_count):
    shards = lax.axis_size("seq")
    heads = lax.axis_size("head")
    blocks = block_list.shape[1] // shards
    s = lax.axis_index("seq")
    h = lax.axis_index("head")
    width = block_list.shape[2]
    entries = lax.dynamic_slice(block_list, (h, s * blocks, 0), (1, blocks, width))[0]
    counts = lax.dynamic_slice(block_count, (h, s * blocks), (1, blocks))[0]
    query_local, table = gather(queries, keys, values, shards, heads)
    attended = attend(entries, counts, query_local, table)
    return give_back(attended, heads)


def solution(mesh):
    placed = (
        P(("seq", "head"), None),
        P(("seq", "head"), None),
        P(("seq", "head"), None),
        P(),
        P(),
    )
    return jax.shard_map(
        per_device, mesh=mesh, in_specs=placed, out_specs=P(("seq", "head"), None), check_vma=False
    )
```

```python
import functools
import math

import jax
import jax.numpy as jnp
from jax import lax
from jax.experimental import pallas as pl
from jax.experimental.pallas import tpu as pltpu
from jax.sharding import PartitionSpec as P

HEADS = 64
KV_HEADS = 8
HEAD_DIM = 128
BLOCK = 128
GROUP = 8
EARLY_PART = (10, 24)
LAG = 2
CORES = 2
HALVES = 2
MESH = pl.DeviceIdType.MESH
OWN, RING, EARLY, CROSS, MATE, MATE_EARLY, MATE_CROSS = range(7)


def gather_kernel(
    shards, heads, q_ref, k_ref, v_ref, qo_ref, tab_ref, kv_send, kv_recv, q_send, q_recv, send, recv, local
):
    rows = k_ref.shape[0]
    per_shard = tab_ref.shape[2]
    q_cols = q_ref.shape[1] // heads
    depth = shards // (CORES * HALVES)
    far = depth // 2
    early_rows = per_shard * EARLY_PART[0] // EARLY_PART[1]
    s = lax.axis_index("seq")
    h = lax.axis_index("head")
    core = s % CORES
    z = (s // CORES) % depth
    half = s // (CORES * depth)

    def seq_at(half_at, z_at):
        return (half_at * depth + z_at) * CORES + core

    up = seq_at(half, (z + 1) % depth)
    down = seq_at(half, (z + depth - 1) % depth)
    mate = s + 1 - 2 * core
    across = seq_at(1 - half, z)
    here = pl.ds(pl.multiple_of(h * rows, 16), rows)

    barrier = pltpu.get_barrier_semaphore()
    for d in range(1, heads):
        pl.semaphore_signal(barrier, inc=1, device_id=(s, (h + d) % heads), device_id_type=MESH)
    for other in (up, down, mate, across):
        pl.semaphore_signal(barrier, inc=1, device_id=(other, h), device_id_type=MESH)
    pl.semaphore_wait(barrier, heads + 3)

    def remote(src, dst, send_sem, recv_sem, to):
        return pltpu.make_async_remote_copy(
            src_ref=src, dst_ref=dst, send_sem=send_sem, recv_sem=recv_sem, device_id=to, device_id_type=MESH
        )

    kv_copies, q_copies = [], []
    for d in range(1, heads):
        peer = (h + d) % heads
        cols = pl.ds(pl.multiple_of(peer * HEAD_DIM, HEAD_DIM), HEAD_DIM)
        for i, ref in enumerate((k_ref, v_ref)):
            kv_copies.append(
                remote(ref.at[:, cols], tab_ref.at[s, i, here], kv_send.at[i, d], kv_recv.at[i, d], (s, peer))
            )
        wide = pl.ds(pl.multiple_of(peer * q_cols, HEAD_DIM), q_cols)
        q_copies.append(remote(q_ref.at[:, wide], qo_ref.at[here], q_send.at[d], q_recv.at[d], (s, peer)))
    cols = pl.ds(pl.multiple_of(h * HEAD_DIM, HEAD_DIM), HEAD_DIM)
    wide = pl.ds(pl.multiple_of(h * q_cols, HEAD_DIM), q_cols)
    kv_local = [
        pltpu.make_async_copy(ref.at[:, cols], tab_ref.at[s, i, here], local.at[i])
        for i, ref in enumerate((k_ref, v_ref))
    ]
    q_local = pltpu.make_async_copy(q_ref.at[:, wide], qo_ref.at[here], local.at[2])
    for copy in kv_copies + kv_local:
        copy.start()
    for copy in kv_local:
        copy.wait()
    for copy in kv_copies:
        copy.wait_recv()

    def flow(mine):
        sent = []

        def copy_of(kind, way, slot, hops, other=False):
            z_at = (z - hops + depth) % depth if way == 0 else (z + hops) % depth
            half_at = mine if kind in (RING, MATE) else 0
            at = (half_at * depth + z_at) * CORES + (1 - core if other else core)
            if kind in (EARLY, MATE_EARLY, OWN):
                span = pl.ds(0, early_rows)
            elif kind in (CROSS, MATE_CROSS):
                span = pl.ds(early_rows, per_shard - early_rows)
            else:
                span = pl.ds(0, per_shard)
            ref = tab_ref.at[at, way, span] if slot == far else tab_ref.at[at, :, span]
            to = {RING: (up, down)[way], EARLY: (up, down)[way], OWN: across, CROSS: across}.get(kind, mate)
            return remote(ref, ref, send.at[kind, way, slot], recv.at[kind, way, slot], (to, h))

        def go(kind, way, hops):
            copy = copy_of(kind, way, hops + 1 if kind in (RING, EARLY) else hops, hops)
            copy.start()
            sent.append(copy)

        def arrive(kind, way, slot):
            copy_of(kind, way, slot, slot, kind in (MATE, MATE_EARLY, MATE_CROSS)).wait_recv()

        stages = [(0, 0)] + [(t, way) for t in range(1, far + 1) for way in (0, 1)]
        for way in (0, 1):
            go(RING, way, 0)
        if mine == 0:
            go(OWN, 0, 0)
            go(CROSS, 0, 0)
        go(MATE, 0, 0)
        for copy in q_copies + [q_local]:
            copy.start()
        if mine == 1:
            arrive(OWN, 0, 0)
            for way in (0, 1):
                go(EARLY, way, 0)
            go(MATE_EARLY, 0, 0)
        pending = [(0, 0)]
        for t in range(1, far + 1):
            for way in (0, 1):
                arrive(RING, way, t)
                if t < far:
                    go(RING, way, t)
            if mine == 1:
                for way in (0, 1):
                    arrive(EARLY, way, t)
                    if t < far:
                        go(EARLY, way, t)
            for way in (0, 1):
                if mine == 0:
                    go(CROSS, way, t)
                go(MATE, way, t)
                if mine == 1:
                    go(MATE_EARLY, way, t)
            if mine == 1:
                while pending and pending[0][0] < t - LAG:
                    at_t, at_way = pending.pop(0)
                    arrive(CROSS, at_way, at_t)
                    go(MATE_CROSS, at_way, at_t)
                pending += [(t, 0), (t, 1)]
        if mine == 1:
            for at_t, at_way in pending:
                arrive(CROSS, at_way, at_t)
                go(MATE_CROSS, at_way, at_t)
        for t, way in stages:
            arrive(MATE, way, t)
            if mine == 1:
                arrive(MATE_EARLY, way, t)
                arrive(MATE_CROSS, way, t)
        for copy in sent:
            copy.wait_send()

    @pl.when(half == 0)
    def _():
        flow(0)

    @pl.when(half == 1)
    def _():
        flow(1)

    for copy in kv_copies:
        copy.wait_send()
    q_local.wait()
    for copy in q_copies:
        copy.wait()


def gather(queries, keys, values, shards, heads):
    rows = queries.shape[0]
    depth = shards // (CORES * HALVES)
    far = depth // 2
    in_hbm = pl.BlockSpec(memory_space=pltpu.HBM)
    dma = pltpu.SemaphoreType.DMA
    return pl.pallas_call(
        functools.partial(gather_kernel, shards, heads),
        out_shape=(
            jax.ShapeDtypeStruct((rows * heads, queries.shape[1] // heads), jnp.bfloat16),
            jax.ShapeDtypeStruct((shards, 2, rows * heads, HEAD_DIM), jnp.bfloat16),
        ),
        in_specs=[in_hbm] * 3,
        out_specs=(pl.BlockSpec(memory_space=pltpu.VMEM),) * 2,
        scratch_shapes=[
            dma((2, heads)),
            dma((2, heads)),
            dma((heads,)),
            dma((heads,)),
            dma((7, 2, far + 1)),
            dma((7, 2, far + 1)),
            dma((3,)),
        ],
        compiler_params=pltpu.CompilerParams(collective_id=0, has_side_effects=True, vmem_limit_bytes=24 * 1024 * 1024),
    )(queries, keys, values)


def attend_kernel(list_ref, count_ref, q_ref, tab_ref, o_ref, qt_ref, m_ref, acc_ref):
    blocks = q_ref.shape[0] // BLOCK
    per_kv = q_ref.shape[1] // HEAD_DIM
    scale = math.log2(math.e) / math.sqrt(HEAD_DIM)
    first = lax.axis_index("seq") * blocks

    def head_cols(head):
        return pl.ds(head * HEAD_DIM, HEAD_DIM)

    @pl.loop(0, blocks)
    def _(b):
        query_rows = pl.ds(pl.multiple_of(b * BLOCK, BLOCK), BLOCK)
        count = count_ref[b]
        groups = (count + GROUP - 1) // GROUP
        for head in range(per_kv):
            qt_ref[:, head * BLOCK : (head + 1) * BLOCK] = q_ref[query_rows, head_cols(head)].T
        m_ref[...] = jnp.full(m_ref.shape, -1e30, jnp.float32)
        acc_ref[...] = jnp.zeros(acc_ref.shape, jnp.float32)

        def listed(g, i):
            parts = []
            for j in range(GROUP):
                at = g * GROUP + j
                entry = jnp.where(at < count, list_ref[b, at], first)
                rows = pl.ds(pl.multiple_of((entry % blocks) * BLOCK, BLOCK), BLOCK)
                parts.append(tab_ref[entry // blocks, i, rows])
            return jnp.concatenate(parts, axis=0)

        def update(g, masked):
            k = listed(g, 0)
            v = listed(g, 1)
            vt = jnp.concatenate([v.T, jnp.ones((16, GROUP * BLOCK), v.dtype)], axis=0)
            scores = jnp.dot(k, qt_ref[...], preferred_element_type=jnp.float32)
            if masked:
                row = lax.broadcasted_iota(jnp.int32, (BLOCK, BLOCK), 1)
                col = lax.broadcasted_iota(jnp.int32, (BLOCK, BLOCK), 0)
                limits = []
                for j in range(GROUP):
                    at = g * GROUP + j
                    limit = jnp.where(list_ref[b, at] == first + b, row, jnp.full_like(row, BLOCK))
                    limit = jnp.where(at < count, limit, jnp.full_like(row, -1))
                    limits.append((limit >= col).astype(jnp.int32))
                allowed = jnp.concatenate(limits, axis=0) > 0
                allowed = jnp.concatenate([allowed] * per_kv, axis=1)
                scores = jnp.where(allowed, scores, jnp.float32(-1e30))
            before = m_ref[:1]
            newest = jnp.maximum(before, jnp.max(scores, axis=0, keepdims=True))
            prob = jnp.exp2(scores * scale - newest * scale).astype(jnp.bfloat16)
            rescale = jnp.exp2(before * scale - newest * scale)
            acc_ref[...] = acc_ref[...] * rescale + jnp.dot(vt, prob, preferred_element_type=jnp.float32)
            m_ref[:1] = newest

        @pl.loop(0, groups)
        def _(g):
            masked = (g + 1) * GROUP > count
            for j in range(GROUP):
                masked = masked | (list_ref[b, g * GROUP + j] == first + b)

            @pl.when(masked)
            def _():
                update(g, True)

            @pl.when(jnp.logical_not(masked))
            def _():
                update(g, False)

        for head in range(per_kv):
            acc = acc_ref[:, head * BLOCK : (head + 1) * BLOCK]
            out = acc[:HEAD_DIM] / acc[HEAD_DIM : HEAD_DIM + 1]
            o_ref[query_rows, head_cols(head)] = out.T.astype(jnp.bfloat16)


def attend(entries, counts, queries, table):
    per_kv = queries.shape[1] // HEAD_DIM
    whole = pl.BlockSpec(memory_space=pltpu.VMEM)
    scalars = pl.BlockSpec(memory_space=pltpu.SMEM)
    return pl.pallas_call(
        attend_kernel,
        out_shape=jax.ShapeDtypeStruct(queries.shape, jnp.bfloat16),
        in_specs=[scalars, scalars, whole, whole],
        out_specs=whole,
        scratch_shapes=[
            pltpu.VMEM((HEAD_DIM, per_kv * BLOCK), jnp.bfloat16),
            pltpu.VMEM((8, per_kv * BLOCK), jnp.float32),
            pltpu.VMEM((HEAD_DIM + 16, per_kv * BLOCK), jnp.float32),
        ],
        compiler_params=pltpu.CompilerParams(vmem_limit_bytes=30 * 1024 * 1024),
    )(entries, counts, queries, table)


def return_kernel(heads, o_ref, out_ref, send, recv, local):
    rows = out_ref.shape[0]
    cols = o_ref.shape[1]
    s = lax.axis_index("seq")
    h = lax.axis_index("head")
    barrier = pltpu.get_barrier_semaphore()
    for d in range(1, heads):
        pl.semaphore_signal(barrier, inc=1, device_id=(s, (h + d) % heads), device_id_type=MESH)
    pl.semaphore_wait(barrier, heads - 1)
    mine = pl.ds(pl.multiple_of(h * cols, HEAD_DIM), cols)
    copies = []
    for d in range(1, heads):
        peer = (h + d) % heads
        copies.append(
            pltpu.make_async_remote_copy(
                src_ref=o_ref.at[pl.ds(pl.multiple_of(peer * rows, 16), rows)],
                dst_ref=out_ref.at[:, mine],
                send_sem=send.at[d],
                recv_sem=recv.at[d],
                device_id=(s, peer),
                device_id_type=MESH,
            )
        )
    own = pltpu.make_async_copy(
        o_ref.at[pl.ds(pl.multiple_of(h * rows, 16), rows)], out_ref.at[:, mine], local
    )
    for copy in copies + [own]:
        copy.start()
    for copy in copies + [own]:
        copy.wait()


def give_back(attended, heads):
    rows, cols = attended.shape
    anywhere = pl.BlockSpec(memory_space=pl.ANY)
    return pl.pallas_call(
        functools.partial(return_kernel, heads),
        out_shape=jax.ShapeDtypeStruct((rows // heads, cols * heads), jnp.bfloat16),
        in_specs=[anywhere],
        out_specs=anywhere,
        scratch_shapes=[
            pltpu.SemaphoreType.DMA((heads,)),
            pltpu.SemaphoreType.DMA((heads,)),
            pltpu.SemaphoreType.DMA,
        ],
        compiler_params=pltpu.CompilerParams(collective_id=1, has_side_effects=True, vmem_limit_bytes=1024 * 1024),
    )(attended)


def per_device(queries, keys, values, block_list, block_count):
    shards = lax.axis_size("seq")
    heads = lax.axis_size("head")
    blocks = block_list.shape[1] // shards
    s = lax.axis_index("seq")
    h = lax.axis_index("head")
    width = block_list.shape[2]
    entries = lax.dynamic_slice(block_list, (h, s * blocks, 0), (1, blocks, width))[0]
    counts = lax.dynamic_slice(block_count, (h, s * blocks), (1, blocks))[0]
    query_local, table = gather(queries, keys, values, shards, heads)
    attended = attend(entries, counts, query_local, table)
    return give_back(attended, heads)


def solution(mesh):
    placed = (
        P(("seq", "head"), None),
        P(("seq", "head"), None),
        P(("seq", "head"), None),
        P(),
        P(),
    )
    return jax.shard_map(
        per_device, mesh=mesh, in_specs=placed, out_specs=P(("seq", "head"), None), check_vma=False
    )
```

```python
import functools
import math

import jax
import jax.numpy as jnp
from jax import lax
from jax.experimental import pallas as pl
from jax.experimental.pallas import tpu as pltpu
from jax.sharding import PartitionSpec as P

HEADS = 64
KV_HEADS = 8
HEAD_DIM = 128
BLOCK = 128
GROUP = 8
CHUNK = 1024
LARGEST = 2.0**40
EARLY_PART = (10, 24)
LAG = 2
CORES = 2
HALVES = 2
MESH = pl.DeviceIdType.MESH
OWN, RING, EARLY, CROSS, MATE, MATE_EARLY, MATE_CROSS = range(7)


def gather_kernel(
    shards, heads, q_ref, k_ref, v_ref, qo_ref, tab_ref, kv_send, kv_recv, q_send, q_recv, send, recv, local
):
    rows = k_ref.shape[0]
    per_shard = tab_ref.shape[2]
    q_cols = q_ref.shape[1] // heads
    depth = shards // (CORES * HALVES)
    far = depth // 2
    early_rows = per_shard * EARLY_PART[0] // EARLY_PART[1]
    s = lax.axis_index("seq")
    h = lax.axis_index("head")
    core = s % CORES
    z = (s // CORES) % depth
    half = s // (CORES * depth)

    def seq_at(half_at, z_at):
        return (half_at * depth + z_at) * CORES + core

    up = seq_at(half, (z + 1) % depth)
    down = seq_at(half, (z + depth - 1) % depth)
    mate = s + 1 - 2 * core
    across = seq_at(1 - half, z)
    here = pl.ds(pl.multiple_of(h * rows, 16), rows)

    barrier = pltpu.get_barrier_semaphore()
    for d in range(1, heads):
        pl.semaphore_signal(barrier, inc=1, device_id=(s, (h + d) % heads), device_id_type=MESH)
    for other in (up, down, mate, across):
        pl.semaphore_signal(barrier, inc=1, device_id=(other, h), device_id_type=MESH)
    pl.semaphore_wait(barrier, heads + 3)

    def remote(src, dst, send_sem, recv_sem, to):
        return pltpu.make_async_remote_copy(
            src_ref=src, dst_ref=dst, send_sem=send_sem, recv_sem=recv_sem, device_id=to, device_id_type=MESH
        )

    kv_copies, q_copies = [], []
    for d in range(1, heads):
        peer = (h + d) % heads
        cols = pl.ds(pl.multiple_of(peer * HEAD_DIM, HEAD_DIM), HEAD_DIM)
        for i, ref in enumerate((k_ref, v_ref)):
            kv_copies.append(
                remote(ref.at[:, cols], tab_ref.at[s, i, here], kv_send.at[i, d], kv_recv.at[i, d], (s, peer))
            )
        wide = pl.ds(pl.multiple_of(peer * q_cols, HEAD_DIM), q_cols)
        q_copies.append(remote(q_ref.at[:, wide], qo_ref.at[here], q_send.at[d], q_recv.at[d], (s, peer)))
    cols = pl.ds(pl.multiple_of(h * HEAD_DIM, HEAD_DIM), HEAD_DIM)
    wide = pl.ds(pl.multiple_of(h * q_cols, HEAD_DIM), q_cols)
    kv_local = [
        pltpu.make_async_copy(ref.at[:, cols], tab_ref.at[s, i, here], local.at[i])
        for i, ref in enumerate((k_ref, v_ref))
    ]
    q_local = pltpu.make_async_copy(q_ref.at[:, wide], qo_ref.at[here], local.at[2])
    for copy in kv_copies + kv_local:
        copy.start()
    for copy in kv_local:
        copy.wait()
    for copy in kv_copies:
        copy.wait_recv()

    def flow(mine):
        sent = []

        def copy_of(kind, way, slot, hops, other=False):
            z_at = (z - hops + depth) % depth if way == 0 else (z + hops) % depth
            half_at = mine if kind in (RING, MATE) else 0
            at = (half_at * depth + z_at) * CORES + (1 - core if other else core)
            if kind in (EARLY, MATE_EARLY, OWN):
                span = pl.ds(0, early_rows)
            elif kind in (CROSS, MATE_CROSS):
                span = pl.ds(early_rows, per_shard - early_rows)
            else:
                span = pl.ds(0, per_shard)
            ref = tab_ref.at[at, way, span] if slot == far else tab_ref.at[at, :, span]
            to = {RING: (up, down)[way], EARLY: (up, down)[way], OWN: across, CROSS: across}.get(kind, mate)
            return remote(ref, ref, send.at[kind, way, slot], recv.at[kind, way, slot], (to, h))

        def needed(kind, way, hops):
            if kind != MATE or hops == 0:
                return None
            return z >= hops if way == 0 else z + hops >= depth

        def guarded(when, act):
            if when is None:
                act()
            else:
                pl.when(when)(act)

        def go(kind, way, hops):
            copy = copy_of(kind, way, hops + 1 if kind in (RING, EARLY) else hops, hops)
            when = needed(kind, way, hops)
            guarded(when, copy.start)
            sent.append((when, copy))

        def arrive(kind, way, slot):
            copy = copy_of(kind, way, slot, slot, kind in (MATE, MATE_EARLY, MATE_CROSS))
            guarded(needed(kind, way, slot), copy.wait_recv)

        stages = [(0, 0)] + [(t, way) for t in range(1, far + 1) for way in (0, 1)]
        for way in (0, 1):
            go(RING, way, 0)
        if mine == 0:
            go(OWN, 0, 0)
            go(CROSS, 0, 0)
        go(MATE, 0, 0)
        for copy in q_copies + [q_local]:
            copy.start()
        if mine == 1:
            arrive(OWN, 0, 0)
            for way in (0, 1):
                go(EARLY, way, 0)
            go(MATE_EARLY, 0, 0)
        pending = [(0, 0)]
        for t in range(1, far + 1):
            for way in (0, 1):
                arrive(RING, way, t)
                if t < far:
                    go(RING, way, t)
            if mine == 1:
                for way in (0, 1):
                    arrive(EARLY, way, t)
                    if t < far:
                        go(EARLY, way, t)
            for way in (0, 1):
                if mine == 0:
                    go(CROSS, way, t)
                go(MATE, way, t)
                if mine == 1:
                    go(MATE_EARLY, way, t)
            if mine == 1:
                while pending and pending[0][0] < t - LAG:
                    at_t, at_way = pending.pop(0)
                    arrive(CROSS, at_way, at_t)
                    go(MATE_CROSS, at_way, at_t)
                pending += [(t, 0), (t, 1)]
        if mine == 1:
            for at_t, at_way in pending:
                arrive(CROSS, at_way, at_t)
                go(MATE_CROSS, at_way, at_t)
        for t, way in stages:
            arrive(MATE, way, t)
            if mine == 1:
                arrive(MATE_EARLY, way, t)
                arrive(MATE_CROSS, way, t)
        for when, copy in sent:
            guarded(when, copy.wait_send)

    @pl.when(half == 0)
    def _():
        flow(0)

    @pl.when(half == 1)
    def _():
        flow(1)

    for copy in kv_copies:
        copy.wait_send()
    q_local.wait()
    for copy in q_copies:
        copy.wait()


def gather(queries, keys, values, shards, heads):
    rows = queries.shape[0]
    depth = shards // (CORES * HALVES)
    far = depth // 2
    in_hbm = pl.BlockSpec(memory_space=pltpu.HBM)
    dma = pltpu.SemaphoreType.DMA
    return pl.pallas_call(
        functools.partial(gather_kernel, shards, heads),
        out_shape=(
            jax.ShapeDtypeStruct((rows * heads, queries.shape[1] // heads), jnp.bfloat16),
            jax.ShapeDtypeStruct((shards, 2, rows * heads, HEAD_DIM), jnp.bfloat16),
        ),
        in_specs=[in_hbm] * 3,
        out_specs=(pl.BlockSpec(memory_space=pltpu.VMEM),) * 2,
        scratch_shapes=[
            dma((2, heads)),
            dma((2, heads)),
            dma((heads,)),
            dma((heads,)),
            dma((7, 2, far + 1)),
            dma((7, 2, far + 1)),
            dma((3,)),
        ],
        compiler_params=pltpu.CompilerParams(collective_id=0, has_side_effects=True, vmem_limit_bytes=24 * 1024 * 1024),
    )(queries, keys, values)


def attend_kernel(list_ref, count_ref, q_ref, tab_ref, o_ref, qt_ref, m_ref, acc_ref):
    blocks = q_ref.shape[0] // BLOCK
    per_kv = q_ref.shape[1] // HEAD_DIM
    columns = per_kv * BLOCK
    scale = math.log2(math.e) / math.sqrt(HEAD_DIM)
    first = lax.axis_index("seq") * blocks

    def head_cols(head):
        return pl.ds(head * HEAD_DIM, HEAD_DIM)

    @pl.loop(0, blocks)
    def _(b):
        query_rows = pl.ds(pl.multiple_of(b * BLOCK, BLOCK), BLOCK)
        count = count_ref[b]
        groups = (count + GROUP - 1) // GROUP
        for head in range(per_kv):
            qt_ref[:, head * BLOCK : (head + 1) * BLOCK] = q_ref[query_rows, head_cols(head)].T

        def listed(at, i):
            entry = jnp.where(at < count, list_ref[b, at], first)
            rows = pl.ds(pl.multiple_of((entry % blocks) * BLOCK, BLOCK), BLOCK)
            return tab_ref[entry // blocks, i, rows]

        def listed_group(g, i):
            return jnp.concatenate([listed(g * GROUP + j, i) for j in range(GROUP)], axis=0)

        def allowed(at):
            row = lax.broadcasted_iota(jnp.int32, (BLOCK, BLOCK), 1)
            col = lax.broadcasted_iota(jnp.int32, (BLOCK, BLOCK), 0)
            limit = jnp.where(list_ref[b, at] == first + b, row, jnp.full_like(row, BLOCK))
            limit = jnp.where(at < count, limit, jnp.full_like(row, -1))
            return (limit >= col).astype(jnp.int32)

        def allowed_group(g, heads):
            parts = jnp.concatenate([allowed(g * GROUP + j) for j in range(GROUP)], axis=0)
            return jnp.concatenate([parts] * heads, axis=1) > 0

        def with_ones(v):
            return jnp.concatenate([v.T, jnp.ones((16, v.shape[0]), v.dtype)], axis=0)

        scores = jnp.dot(listed(0, 0), qt_ref[...], preferred_element_type=jnp.float32)
        start = jnp.concatenate([allowed(0)] * per_kv, axis=1) > 0
        scores = jnp.where(start, scores, jnp.float32(-1e30))
        m_ref[:1] = jnp.max(scores, axis=0, keepdims=True)
        acc_ref[0] = jnp.zeros(acc_ref.shape[1:], jnp.float32)

        def update(g, masked):
            k = listed_group(g, 0)
            vt = with_ones(listed_group(g, 1))
            for c in range(columns // CHUNK):
                cols = pl.ds(c * CHUNK, CHUNK)
                scores = jnp.dot(k, qt_ref[:, cols], preferred_element_type=jnp.float32)
                if masked:
                    scores = jnp.where(allowed_group(g, CHUNK // BLOCK), scores, jnp.float32(-1e30))
                prob = jnp.exp2(scores * scale - m_ref[:1, cols] * scale).astype(jnp.bfloat16)
                acc_ref[(g + 1) % 2, :, cols] = acc_ref[g % 2, :, cols] + jnp.dot(
                    vt, prob, preferred_element_type=jnp.float32
                )

        def rescaled_update(g):
            k = listed_group(g, 0)
            vt = with_ones(listed_group(g, 1))
            for c in range(columns // CHUNK):
                cols = pl.ds(c * CHUNK, CHUNK)
                scores = jnp.dot(k, qt_ref[:, cols], preferred_element_type=jnp.float32)
                scores = jnp.where(allowed_group(g, CHUNK // BLOCK), scores, jnp.float32(-1e30))
                before = m_ref[:1, cols]
                newest = jnp.maximum(before, jnp.max(scores, axis=0, keepdims=True))
                prob = jnp.exp2(scores * scale - newest * scale).astype(jnp.bfloat16)
                rescale = jnp.exp2(before * scale - newest * scale)
                acc_ref[(g + 1) % 2, :, cols] = acc_ref[g % 2, :, cols] * rescale + jnp.dot(
                    vt, prob, preferred_element_type=jnp.float32
                )
                m_ref[:1, cols] = newest

        @pl.loop(0, groups)
        def _(g):
            masked = (g + 1) * GROUP > count
            for j in range(GROUP):
                masked = masked | (list_ref[b, g * GROUP + j] == first + b)

            @pl.when(masked)
            def _():
                update(g, True)

            @pl.when(jnp.logical_not(masked))
            def _():
                update(g, False)

            sums = acc_ref[(g + 1) % 2, HEAD_DIM : HEAD_DIM + 1]
            fits = jnp.min(jnp.where(sums < LARGEST, 1.0, 0.0)) > 0.5

            @pl.when(jnp.logical_not(fits))
            def _():
                rescaled_update(g)

        for head in range(per_kv):
            acc = acc_ref[groups % 2, :, head * BLOCK : (head + 1) * BLOCK]
            out = acc[:HEAD_DIM] / acc[HEAD_DIM : HEAD_DIM + 1]
            o_ref[query_rows, head_cols(head)] = out.T.astype(jnp.bfloat16)


def attend(entries, counts, queries, table):
    per_kv = queries.shape[1] // HEAD_DIM
    whole = pl.BlockSpec(memory_space=pltpu.VMEM)
    scalars = pl.BlockSpec(memory_space=pltpu.SMEM)
    return pl.pallas_call(
        attend_kernel,
        out_shape=jax.ShapeDtypeStruct(queries.shape, jnp.bfloat16),
        in_specs=[scalars, scalars, whole, whole],
        out_specs=whole,
        scratch_shapes=[
            pltpu.VMEM((HEAD_DIM, per_kv * BLOCK), jnp.bfloat16),
            pltpu.VMEM((8, per_kv * BLOCK), jnp.float32),
            pltpu.VMEM((2, HEAD_DIM + 16, per_kv * BLOCK), jnp.float32),
        ],
        compiler_params=pltpu.CompilerParams(vmem_limit_bytes=30 * 1024 * 1024),
    )(entries, counts, queries, table)


def return_kernel(heads, o_ref, out_ref, send, recv, local):
    rows = out_ref.shape[0]
    cols = o_ref.shape[1]
    s = lax.axis_index("seq")
    h = lax.axis_index("head")
    barrier = pltpu.get_barrier_semaphore()
    for d in range(1, heads):
        pl.semaphore_signal(barrier, inc=1, device_id=(s, (h + d) % heads), device_id_type=MESH)
    pl.semaphore_wait(barrier, heads - 1)
    mine = pl.ds(pl.multiple_of(h * cols, HEAD_DIM), cols)
    copies = []
    for d in range(1, heads):
        peer = (h + d) % heads
        copies.append(
            pltpu.make_async_remote_copy(
                src_ref=o_ref.at[pl.ds(pl.multiple_of(peer * rows, 16), rows)],
                dst_ref=out_ref.at[:, mine],
                send_sem=send.at[d],
                recv_sem=recv.at[d],
                device_id=(s, peer),
                device_id_type=MESH,
            )
        )
    own = pltpu.make_async_copy(
        o_ref.at[pl.ds(pl.multiple_of(h * rows, 16), rows)], out_ref.at[:, mine], local
    )
    for copy in copies + [own]:
        copy.start()
    for copy in copies + [own]:
        copy.wait()


def give_back(attended, heads):
    rows, cols = attended.shape
    anywhere = pl.BlockSpec(memory_space=pl.ANY)
    return pl.pallas_call(
        functools.partial(return_kernel, heads),
        out_shape=jax.ShapeDtypeStruct((rows // heads, cols * heads), jnp.bfloat16),
        in_specs=[anywhere],
        out_specs=anywhere,
        scratch_shapes=[
            pltpu.SemaphoreType.DMA((heads,)),
            pltpu.SemaphoreType.DMA((heads,)),
            pltpu.SemaphoreType.DMA,
        ],
        compiler_params=pltpu.CompilerParams(collective_id=1, has_side_effects=True, vmem_limit_bytes=1024 * 1024),
    )(attended)


def per_device(queries, keys, values, block_list, block_count):
    shards = lax.axis_size("seq")
    heads = lax.axis_size("head")
    blocks = block_list.shape[1] // shards
    s = lax.axis_index("seq")
    h = lax.axis_index("head")
    width = block_list.shape[2]
    entries = lax.dynamic_slice(block_list, (h, s * blocks, 0), (1, blocks, width))[0]
    counts = lax.dynamic_slice(block_count, (h, s * blocks), (1, blocks))[0]
    query_local, table = gather(queries, keys, values, shards, heads)
    attended = attend(entries, counts, query_local, table)
    return give_back(attended, heads)


def solution(mesh):
    placed = (
        P(("seq", "head"), None),
        P(("seq", "head"), None),
        P(("seq", "head"), None),
        P(),
        P(),
    )
    return jax.shard_map(
        per_device, mesh=mesh, in_specs=placed, out_specs=P(("seq", "head"), None), check_vma=False
    )
```

```python
import functools
import math

import jax
import jax.numpy as jnp
from jax import lax
from jax.experimental import pallas as pl
from jax.experimental.pallas import tpu as pltpu
from jax.sharding import PartitionSpec as P

HEADS = 64
KV_HEADS = 8
HEAD_DIM = 128
BLOCK = 128
GROUP = 16
CHUNK = 1024
LARGEST = 2.0**40
EARLY_PART = (10, 24)
LAG = 2
CORES = 2
HALVES = 2
MESH = pl.DeviceIdType.MESH
OWN, RING, EARLY, CROSS, MATE, MATE_EARLY, MATE_CROSS = range(7)


def gather_kernel(
    shards, heads, q_ref, k_ref, v_ref, qo_ref, tab_ref, kv_send, kv_recv, q_send, q_recv, send, recv, local
):
    rows = k_ref.shape[0]
    per_shard = tab_ref.shape[2]
    q_cols = q_ref.shape[1] // heads
    depth = shards // (CORES * HALVES)
    far = depth // 2
    early_rows = per_shard * EARLY_PART[0] // EARLY_PART[1]
    s = lax.axis_index("seq")
    h = lax.axis_index("head")
    core = s % CORES
    z = (s // CORES) % depth
    half = s // (CORES * depth)

    def seq_at(half_at, z_at):
        return (half_at * depth + z_at) * CORES + core

    up = seq_at(half, (z + 1) % depth)
    down = seq_at(half, (z + depth - 1) % depth)
    mate = s + 1 - 2 * core
    across = seq_at(1 - half, z)
    here = pl.ds(pl.multiple_of(h * rows, 16), rows)

    barrier = pltpu.get_barrier_semaphore()
    for d in range(1, heads):
        pl.semaphore_signal(barrier, inc=1, device_id=(s, (h + d) % heads), device_id_type=MESH)
    for other in (up, down, mate, across):
        pl.semaphore_signal(barrier, inc=1, device_id=(other, h), device_id_type=MESH)
    pl.semaphore_wait(barrier, heads + 3)

    def remote(src, dst, send_sem, recv_sem, to):
        return pltpu.make_async_remote_copy(
            src_ref=src, dst_ref=dst, send_sem=send_sem, recv_sem=recv_sem, device_id=to, device_id_type=MESH
        )

    kv_copies, q_copies = [], []
    for d in range(1, heads):
        peer = (h + d) % heads
        cols = pl.ds(pl.multiple_of(peer * HEAD_DIM, HEAD_DIM), HEAD_DIM)
        for i, ref in enumerate((k_ref, v_ref)):
            kv_copies.append(
                remote(ref.at[:, cols], tab_ref.at[s, i, here], kv_send.at[i, d], kv_recv.at[i, d], (s, peer))
            )
        wide = pl.ds(pl.multiple_of(peer * q_cols, HEAD_DIM), q_cols)
        q_copies.append(remote(q_ref.at[:, wide], qo_ref.at[here], q_send.at[d], q_recv.at[d], (s, peer)))
    cols = pl.ds(pl.multiple_of(h * HEAD_DIM, HEAD_DIM), HEAD_DIM)
    wide = pl.ds(pl.multiple_of(h * q_cols, HEAD_DIM), q_cols)
    kv_local = [
        pltpu.make_async_copy(ref.at[:, cols], tab_ref.at[s, i, here], local.at[i])
        for i, ref in enumerate((k_ref, v_ref))
    ]
    q_local = pltpu.make_async_copy(q_ref.at[:, wide], qo_ref.at[here], local.at[2])
    for copy in kv_copies + kv_local:
        copy.start()
    for copy in kv_local:
        copy.wait()
    for copy in kv_copies:
        copy.wait_recv()

    def flow(mine):
        sent = []

        def copy_of(kind, way, slot, hops, other=False):
            z_at = (z - hops + depth) % depth if way == 0 else (z + hops) % depth
            half_at = mine if kind in (RING, MATE) else 0
            at = (half_at * depth + z_at) * CORES + (1 - core if other else core)
            if kind in (EARLY, MATE_EARLY, OWN):
                span = pl.ds(0, early_rows)
            elif kind in (CROSS, MATE_CROSS):
                span = pl.ds(early_rows, per_shard - early_rows)
            else:
                span = pl.ds(0, per_shard)
            ref = tab_ref.at[at, way, span] if slot == far else tab_ref.at[at, :, span]
            to = {RING: (up, down)[way], EARLY: (up, down)[way], OWN: across, CROSS: across}.get(kind, mate)
            return remote(ref, ref, send.at[kind, way, slot], recv.at[kind, way, slot], (to, h))

        def needed(kind, way, hops):
            if kind != MATE or hops == 0:
                return None
            return z >= hops if way == 0 else z + hops >= depth

        def guarded(when, act):
            if when is None:
                act()
            else:
                pl.when(when)(act)

        def go(kind, way, hops):
            copy = copy_of(kind, way, hops + 1 if kind in (RING, EARLY) else hops, hops)
            when = needed(kind, way, hops)
            guarded(when, copy.start)
            sent.append((when, copy))

        def arrive(kind, way, slot):
            copy = copy_of(kind, way, slot, slot, kind in (MATE, MATE_EARLY, MATE_CROSS))
            guarded(needed(kind, way, slot), copy.wait_recv)

        stages = [(0, 0)] + [(t, way) for t in range(1, far + 1) for way in (0, 1)]
        for way in (0, 1):
            go(RING, way, 0)
        if mine == 0:
            go(OWN, 0, 0)
            go(CROSS, 0, 0)
        go(MATE, 0, 0)
        for copy in q_copies + [q_local]:
            copy.start()
        if mine == 1:
            arrive(OWN, 0, 0)
            for way in (0, 1):
                go(EARLY, way, 0)
            go(MATE_EARLY, 0, 0)
        pending = [(0, 0)]
        for t in range(1, far + 1):
            for way in (0, 1):
                arrive(RING, way, t)
                if t < far:
                    go(RING, way, t)
            if mine == 1:
                for way in (0, 1):
                    arrive(EARLY, way, t)
                    if t < far:
                        go(EARLY, way, t)
            for way in (0, 1):
                if mine == 0:
                    go(CROSS, way, t)
                go(MATE, way, t)
                if mine == 1:
                    go(MATE_EARLY, way, t)
            if mine == 1:
                while pending and pending[0][0] < t - LAG:
                    at_t, at_way = pending.pop(0)
                    arrive(CROSS, at_way, at_t)
                    go(MATE_CROSS, at_way, at_t)
                pending += [(t, 0), (t, 1)]
        if mine == 1:
            for at_t, at_way in pending:
                arrive(CROSS, at_way, at_t)
                go(MATE_CROSS, at_way, at_t)
        for t, way in stages:
            arrive(MATE, way, t)
            if mine == 1:
                arrive(MATE_EARLY, way, t)
                arrive(MATE_CROSS, way, t)
        for when, copy in sent:
            guarded(when, copy.wait_send)

    @pl.when(half == 0)
    def _():
        flow(0)

    @pl.when(half == 1)
    def _():
        flow(1)

    for copy in kv_copies:
        copy.wait_send()
    q_local.wait()
    for copy in q_copies:
        copy.wait()


def gather(queries, keys, values, shards, heads):
    rows = queries.shape[0]
    depth = shards // (CORES * HALVES)
    far = depth // 2
    in_hbm = pl.BlockSpec(memory_space=pltpu.HBM)
    dma = pltpu.SemaphoreType.DMA
    return pl.pallas_call(
        functools.partial(gather_kernel, shards, heads),
        out_shape=(
            jax.ShapeDtypeStruct((rows * heads, queries.shape[1] // heads), jnp.bfloat16),
            jax.ShapeDtypeStruct((shards, 2, rows * heads, HEAD_DIM), jnp.bfloat16),
        ),
        in_specs=[in_hbm] * 3,
        out_specs=(pl.BlockSpec(memory_space=pltpu.VMEM),) * 2,
        scratch_shapes=[
            dma((2, heads)),
            dma((2, heads)),
            dma((heads,)),
            dma((heads,)),
            dma((7, 2, far + 1)),
            dma((7, 2, far + 1)),
            dma((3,)),
        ],
        compiler_params=pltpu.CompilerParams(collective_id=0, has_side_effects=True, vmem_limit_bytes=24 * 1024 * 1024),
    )(queries, keys, values)


def attend_kernel(list_ref, count_ref, q_ref, tab_ref, o_ref, qt_ref, m_ref, acc_ref):
    blocks = q_ref.shape[0] // BLOCK
    per_kv = q_ref.shape[1] // HEAD_DIM
    columns = per_kv * BLOCK
    scale = math.log2(math.e) / math.sqrt(HEAD_DIM)
    first = lax.axis_index("seq") * blocks

    def head_cols(head):
        return pl.ds(head * HEAD_DIM, HEAD_DIM)

    @pl.loop(0, blocks)
    def _(b):
        query_rows = pl.ds(pl.multiple_of(b * BLOCK, BLOCK), BLOCK)
        count = count_ref[b]
        groups = (count + GROUP - 1) // GROUP
        for head in range(per_kv):
            qt_ref[:, head * BLOCK : (head + 1) * BLOCK] = q_ref[query_rows, head_cols(head)].T

        def listed(at, i):
            entry = jnp.where(at < count, list_ref[b, at], first)
            rows = pl.ds(pl.multiple_of((entry % blocks) * BLOCK, BLOCK), BLOCK)
            return tab_ref[entry // blocks, i, rows]

        def listed_group(g, i):
            return jnp.concatenate([listed(g * GROUP + j, i) for j in range(GROUP)], axis=0)

        def allowed(at):
            row = lax.broadcasted_iota(jnp.int32, (BLOCK, BLOCK), 1)
            col = lax.broadcasted_iota(jnp.int32, (BLOCK, BLOCK), 0)
            limit = jnp.where(list_ref[b, at] == first + b, row, jnp.full_like(row, BLOCK))
            limit = jnp.where(at < count, limit, jnp.full_like(row, -1))
            return (limit >= col).astype(jnp.int32)

        def allowed_group(g, heads):
            parts = jnp.concatenate([allowed(g * GROUP + j) for j in range(GROUP)], axis=0)
            return jnp.concatenate([parts] * heads, axis=1) > 0

        def with_ones(v):
            return jnp.concatenate([v.T, jnp.ones((16, v.shape[0]), v.dtype)], axis=0)

        scores = jnp.dot(listed(0, 0), qt_ref[...], preferred_element_type=jnp.float32)
        start = jnp.concatenate([allowed(0)] * per_kv, axis=1) > 0
        scores = jnp.where(start, scores, jnp.float32(-1e30))
        m_ref[:1] = jnp.max(scores, axis=0, keepdims=True)
        acc_ref[0] = jnp.zeros(acc_ref.shape[1:], jnp.float32)

        def update(g, masked):
            k = listed_group(g, 0)
            vt = with_ones(listed_group(g, 1))
            for c in range(columns // CHUNK):
                cols = pl.ds(c * CHUNK, CHUNK)
                scores = jnp.dot(k, qt_ref[:, cols], preferred_element_type=jnp.float32)
                if masked:
                    scores = jnp.where(allowed_group(g, CHUNK // BLOCK), scores, jnp.float32(-1e30))
                prob = jnp.exp2(scores * scale - m_ref[:1, cols] * scale).astype(jnp.bfloat16)
                acc_ref[(g + 1) % 2, :, cols] = acc_ref[g % 2, :, cols] + jnp.dot(
                    vt, prob, preferred_element_type=jnp.float32
                )

        def rescaled_update(g):
            k = listed_group(g, 0)
            vt = with_ones(listed_group(g, 1))
            for c in range(columns // CHUNK):
                cols = pl.ds(c * CHUNK, CHUNK)
                scores = jnp.dot(k, qt_ref[:, cols], preferred_element_type=jnp.float32)
                scores = jnp.where(allowed_group(g, CHUNK // BLOCK), scores, jnp.float32(-1e30))
                before = m_ref[:1, cols]
                newest = jnp.maximum(before, jnp.max(scores, axis=0, keepdims=True))
                prob = jnp.exp2(scores * scale - newest * scale).astype(jnp.bfloat16)
                rescale = jnp.exp2(before * scale - newest * scale)
                acc_ref[(g + 1) % 2, :, cols] = acc_ref[g % 2, :, cols] * rescale + jnp.dot(
                    vt, prob, preferred_element_type=jnp.float32
                )
                m_ref[:1, cols] = newest

        @pl.loop(0, groups)
        def _(g):
            masked = (g + 1) * GROUP > count
            for j in range(GROUP):
                masked = masked | (list_ref[b, g * GROUP + j] == first + b)

            @pl.when(masked)
            def _():
                update(g, True)

            @pl.when(jnp.logical_not(masked))
            def _():
                update(g, False)

            sums = acc_ref[(g + 1) % 2, HEAD_DIM : HEAD_DIM + 1]
            fits = jnp.min(jnp.where(sums < LARGEST, 1.0, 0.0)) > 0.5

            @pl.when(jnp.logical_not(fits))
            def _():
                rescaled_update(g)

        for head in range(per_kv):
            acc = acc_ref[groups % 2, :, head * BLOCK : (head + 1) * BLOCK]
            out = acc[:HEAD_DIM] / acc[HEAD_DIM : HEAD_DIM + 1]
            o_ref[query_rows, head_cols(head)] = out.T.astype(jnp.bfloat16)


def attend(entries, counts, queries, table):
    per_kv = queries.shape[1] // HEAD_DIM
    whole = pl.BlockSpec(memory_space=pltpu.VMEM)
    scalars = pl.BlockSpec(memory_space=pltpu.SMEM)
    return pl.pallas_call(
        attend_kernel,
        out_shape=jax.ShapeDtypeStruct(queries.shape, jnp.bfloat16),
        in_specs=[scalars, scalars, whole, whole],
        out_specs=whole,
        scratch_shapes=[
            pltpu.VMEM((HEAD_DIM, per_kv * BLOCK), jnp.bfloat16),
            pltpu.VMEM((8, per_kv * BLOCK), jnp.float32),
            pltpu.VMEM((2, HEAD_DIM + 16, per_kv * BLOCK), jnp.float32),
        ],
        compiler_params=pltpu.CompilerParams(vmem_limit_bytes=30 * 1024 * 1024),
    )(entries, counts, queries, table)


def return_kernel(heads, o_ref, out_ref, send, recv, local):
    rows = out_ref.shape[0]
    cols = o_ref.shape[1]
    s = lax.axis_index("seq")
    h = lax.axis_index("head")
    barrier = pltpu.get_barrier_semaphore()
    for d in range(1, heads):
        pl.semaphore_signal(barrier, inc=1, device_id=(s, (h + d) % heads), device_id_type=MESH)
    pl.semaphore_wait(barrier, heads - 1)
    mine = pl.ds(pl.multiple_of(h * cols, HEAD_DIM), cols)
    copies = []
    for d in range(1, heads):
        peer = (h + d) % heads
        copies.append(
            pltpu.make_async_remote_copy(
                src_ref=o_ref.at[pl.ds(pl.multiple_of(peer * rows, 16), rows)],
                dst_ref=out_ref.at[:, mine],
                send_sem=send.at[d],
                recv_sem=recv.at[d],
                device_id=(s, peer),
                device_id_type=MESH,
            )
        )
    own = pltpu.make_async_copy(
        o_ref.at[pl.ds(pl.multiple_of(h * rows, 16), rows)], out_ref.at[:, mine], local
    )
    for copy in copies + [own]:
        copy.start()
    for copy in copies + [own]:
        copy.wait()


def give_back(attended, heads):
    rows, cols = attended.shape
    anywhere = pl.BlockSpec(memory_space=pl.ANY)
    return pl.pallas_call(
        functools.partial(return_kernel, heads),
        out_shape=jax.ShapeDtypeStruct((rows // heads, cols * heads), jnp.bfloat16),
        in_specs=[anywhere],
        out_specs=anywhere,
        scratch_shapes=[
            pltpu.SemaphoreType.DMA((heads,)),
            pltpu.SemaphoreType.DMA((heads,)),
            pltpu.SemaphoreType.DMA,
        ],
        compiler_params=pltpu.CompilerParams(collective_id=1, has_side_effects=True, vmem_limit_bytes=1024 * 1024),
    )(attended)


def per_device(queries, keys, values, block_list, block_count):
    shards = lax.axis_size("seq")
    heads = lax.axis_size("head")
    blocks = block_list.shape[1] // shards
    s = lax.axis_index("seq")
    h = lax.axis_index("head")
    width = block_list.shape[2]
    entries = lax.dynamic_slice(block_list, (h, s * blocks, 0), (1, blocks, width))[0]
    counts = lax.dynamic_slice(block_count, (h, s * blocks), (1, blocks))[0]
    queries, keys, values = (
        pltpu.with_memory_space_constraint(array, pltpu.HBM) for array in (queries, keys, values)
    )
    query_local, table = gather(queries, keys, values, shards, heads)
    attended = attend(entries, counts, query_local, table)
    return give_back(attended, heads)


def solution(mesh):
    placed = (
        P(("seq", "head"), None),
        P(("seq", "head"), None),
        P(("seq", "head"), None),
        P(),
        P(),
    )
    return jax.shard_map(
        per_device, mesh=mesh, in_specs=placed, out_specs=P(("seq", "head"), None), check_vma=False
    )
```

```python
import functools
import math

import jax
import jax.numpy as jnp
from jax import lax
from jax.experimental import pallas as pl
from jax.experimental.pallas import tpu as pltpu
from jax.sharding import PartitionSpec as P

HEADS = 64
KV_HEADS = 8
HEAD_DIM = 128
BLOCK = 128
GROUP = 16
CHUNK = 1024
LARGEST = 2.0**40
EARLY_PART = (10, 24)
LAG = 2
CORES = 2
HALVES = 2
MESH = pl.DeviceIdType.MESH
STEPS = ((1, 2), (1, 1), (1, 3), (1, 0), (0, 2), (0, 1), (0, 3))
OWN, RING, EARLY, CROSS, MATE, MATE_EARLY, MATE_CROSS = range(7)


def peers_of(h, heads):
    half = heads // 2
    return [(d + 1, (h // half + x) % 2 * half + (h % half + y) % half) for d, (x, y) in enumerate(STEPS)]


def gather_kernel(
    shards, heads, q_ref, k_ref, v_ref, qo_ref, tab_ref, kv_send, kv_recv, q_send, q_recv, send, recv, local
):
    rows = k_ref.shape[0]
    per_shard = tab_ref.shape[2]
    q_cols = q_ref.shape[1] // heads
    depth = shards // (CORES * HALVES)
    far = depth // 2
    early_rows = per_shard * EARLY_PART[0] // EARLY_PART[1]
    s = lax.axis_index("seq")
    h = lax.axis_index("head")
    core = s % CORES
    z = (s // CORES) % depth
    half = s // (CORES * depth)

    def seq_at(half_at, z_at):
        return (half_at * depth + z_at) * CORES + core

    up = seq_at(half, (z + 1) % depth)
    down = seq_at(half, (z + depth - 1) % depth)
    mate = s + 1 - 2 * core
    across = seq_at(1 - half, z)
    here = pl.ds(pl.multiple_of(h * rows, 16), rows)

    barrier = pltpu.get_barrier_semaphore()
    for _, peer in peers_of(h, heads):
        pl.semaphore_signal(barrier, inc=1, device_id=(s, peer), device_id_type=MESH)
    for other in (up, down, mate, across):
        pl.semaphore_signal(barrier, inc=1, device_id=(other, h), device_id_type=MESH)
    pl.semaphore_wait(barrier, heads + 3)

    def remote(src, dst, send_sem, recv_sem, to):
        return pltpu.make_async_remote_copy(
            src_ref=src, dst_ref=dst, send_sem=send_sem, recv_sem=recv_sem, device_id=to, device_id_type=MESH
        )

    kv_copies, q_copies = [], []
    for d, peer in peers_of(h, heads):
        cols = pl.ds(pl.multiple_of(peer * HEAD_DIM, HEAD_DIM), HEAD_DIM)
        for i, ref in enumerate((k_ref, v_ref)):
            kv_copies.append(
                remote(ref.at[:, cols], tab_ref.at[s, i, here], kv_send.at[i, d], kv_recv.at[i, d], (s, peer))
            )
        wide = pl.ds(pl.multiple_of(peer * q_cols, HEAD_DIM), q_cols)
        q_copies.append(remote(q_ref.at[:, wide], qo_ref.at[here], q_send.at[d], q_recv.at[d], (s, peer)))
    cols = pl.ds(pl.multiple_of(h * HEAD_DIM, HEAD_DIM), HEAD_DIM)
    wide = pl.ds(pl.multiple_of(h * q_cols, HEAD_DIM), q_cols)
    kv_local = [
        pltpu.make_async_copy(ref.at[:, cols], tab_ref.at[s, i, here], local.at[i])
        for i, ref in enumerate((k_ref, v_ref))
    ]
    q_local = pltpu.make_async_copy(q_ref.at[:, wide], qo_ref.at[here], local.at[2])
    for copy in kv_copies + kv_local:
        copy.start()
    for copy in kv_local:
        copy.wait()
    for copy in kv_copies:
        copy.wait_recv()

    def flow(mine):
        sent = []

        def copy_of(kind, way, slot, hops, other=False):
            z_at = (z - hops + depth) % depth if way == 0 else (z + hops) % depth
            half_at = mine if kind in (RING, MATE) else 0
            at = (half_at * depth + z_at) * CORES + (1 - core if other else core)
            if kind in (EARLY, MATE_EARLY, OWN):
                span = pl.ds(0, early_rows)
            elif kind in (CROSS, MATE_CROSS):
                span = pl.ds(early_rows, per_shard - early_rows)
            else:
                span = pl.ds(0, per_shard)
            ref = tab_ref.at[at, way, span] if slot == far else tab_ref.at[at, :, span]
            to = {RING: (up, down)[way], EARLY: (up, down)[way], OWN: across, CROSS: across}.get(kind, mate)
            return remote(ref, ref, send.at[kind, way, slot], recv.at[kind, way, slot], (to, h))

        def needed(kind, way, hops):
            if hops == 0:
                return None
            if kind == MATE:
                return z >= hops if way == 0 else z + hops >= depth
            if kind == RING and mine == 1:
                return z >= hops if way == 0 else (z + hops) % depth < far
            return None

        def onward(way, hops):
            if mine == 0:
                return None
            return (z >= hops) & (z + 1 < depth) if way == 0 else (z + hops) % depth < far

        def guarded(when, act):
            if when is None:
                act()
            else:
                pl.when(when)(act)

        def go(kind, way, hops):
            copy = copy_of(kind, way, hops + 1 if kind in (RING, EARLY) else hops, hops)
            when = onward(way, hops) if kind == RING else needed(kind, way, hops)
            guarded(when, copy.start)
            sent.append((when, copy))

        def arrive(kind, way, slot):
            copy = copy_of(kind, way, slot, slot, kind in (MATE, MATE_EARLY, MATE_CROSS))
            guarded(needed(kind, way, slot), copy.wait_recv)

        stages = [(0, 0)] + [(t, way) for t in range(1, far + 1) for way in (0, 1)]
        for way in (0, 1):
            go(RING, way, 0)
        if mine == 0:
            go(OWN, 0, 0)
            go(CROSS, 0, 0)
        go(MATE, 0, 0)
        for copy in q_copies + [q_local]:
            copy.start()
        if mine == 1:
            arrive(OWN, 0, 0)
            for way in (0, 1):
                go(EARLY, way, 0)
            go(MATE_EARLY, 0, 0)
        pending = [(0, 0)]
        for t in range(1, far + 1):
            for way in (0, 1):
                arrive(RING, way, t)
                if t < far:
                    go(RING, way, t)
            if mine == 1:
                for way in (0, 1):
                    arrive(EARLY, way, t)
                    if t < far:
                        go(EARLY, way, t)
            for way in (0, 1):
                if mine == 0:
                    go(CROSS, way, t)
                go(MATE, way, t)
                if mine == 1:
                    go(MATE_EARLY, way, t)
            if mine == 1:
                while pending and pending[0][0] < t - LAG:
                    at_t, at_way = pending.pop(0)
                    arrive(CROSS, at_way, at_t)
                    go(MATE_CROSS, at_way, at_t)
                pending += [(t, 0), (t, 1)]
        if mine == 1:
            for at_t, at_way in pending:
                arrive(CROSS, at_way, at_t)
                go(MATE_CROSS, at_way, at_t)
        for t, way in stages:
            arrive(MATE, way, t)
            if mine == 1:
                arrive(MATE_EARLY, way, t)
                arrive(MATE_CROSS, way, t)
        for when, copy in sent:
            guarded(when, copy.wait_send)

    @pl.when(half == 0)
    def _():
        flow(0)

    @pl.when(half == 1)
    def _():
        flow(1)

    for copy in kv_copies:
        copy.wait_send()
    q_local.wait()
    for copy in q_copies:
        copy.wait()


def gather(queries, keys, values, shards, heads):
    rows = queries.shape[0]
    depth = shards // (CORES * HALVES)
    far = depth // 2
    in_hbm = pl.BlockSpec(memory_space=pltpu.HBM)
    dma = pltpu.SemaphoreType.DMA
    return pl.pallas_call(
        functools.partial(gather_kernel, shards, heads),
        out_shape=(
            jax.ShapeDtypeStruct((rows * heads, queries.shape[1] // heads), jnp.bfloat16),
            jax.ShapeDtypeStruct((shards, 2, rows * heads, HEAD_DIM), jnp.bfloat16),
        ),
        in_specs=[in_hbm] * 3,
        out_specs=(pl.BlockSpec(memory_space=pltpu.VMEM),) * 2,
        scratch_shapes=[
            dma((2, heads)),
            dma((2, heads)),
            dma((heads,)),
            dma((heads,)),
            dma((7, 2, far + 1)),
            dma((7, 2, far + 1)),
            dma((3,)),
        ],
        compiler_params=pltpu.CompilerParams(collective_id=0, has_side_effects=True, vmem_limit_bytes=24 * 1024 * 1024),
    )(queries, keys, values)


def attend_kernel(list_ref, count_ref, q_ref, tab_ref, o_ref, qt_ref, m_ref, acc_ref):
    blocks = q_ref.shape[0] // BLOCK
    per_kv = q_ref.shape[1] // HEAD_DIM
    columns = per_kv * BLOCK
    scale = math.log2(math.e) / math.sqrt(HEAD_DIM)
    first = lax.axis_index("seq") * blocks

    def head_cols(head):
        return pl.ds(head * HEAD_DIM, HEAD_DIM)

    @pl.loop(0, blocks)
    def _(b):
        query_rows = pl.ds(pl.multiple_of(b * BLOCK, BLOCK), BLOCK)
        count = count_ref[b]
        groups = (count + GROUP - 1) // GROUP
        for head in range(per_kv):
            qt_ref[:, head * BLOCK : (head + 1) * BLOCK] = q_ref[query_rows, head_cols(head)].T

        def listed(at, i):
            entry = jnp.where(at < count, list_ref[b, at], first)
            rows = pl.ds(pl.multiple_of((entry % blocks) * BLOCK, BLOCK), BLOCK)
            return tab_ref[entry // blocks, i, rows]

        def listed_group(g, i):
            return jnp.concatenate([listed(g * GROUP + j, i) for j in range(GROUP)], axis=0)

        def allowed(at):
            row = lax.broadcasted_iota(jnp.int32, (BLOCK, BLOCK), 1)
            col = lax.broadcasted_iota(jnp.int32, (BLOCK, BLOCK), 0)
            limit = jnp.where(list_ref[b, at] == first + b, row, jnp.full_like(row, BLOCK))
            limit = jnp.where(at < count, limit, jnp.full_like(row, -1))
            return (limit >= col).astype(jnp.int32)

        def allowed_group(g, heads):
            parts = jnp.concatenate([allowed(g * GROUP + j) for j in range(GROUP)], axis=0)
            return jnp.concatenate([parts] * heads, axis=1) > 0

        def with_ones(v):
            return jnp.concatenate([v.T, jnp.ones((16, v.shape[0]), v.dtype)], axis=0)

        scores = jnp.dot(listed(0, 0), qt_ref[...], preferred_element_type=jnp.float32)
        start = jnp.concatenate([allowed(0)] * per_kv, axis=1) > 0
        scores = jnp.where(start, scores, jnp.float32(-1e30))
        m_ref[:1] = jnp.max(scores, axis=0, keepdims=True)
        acc_ref[0] = jnp.zeros(acc_ref.shape[1:], jnp.float32)

        def update(g, masked):
            k = listed_group(g, 0)
            vt = with_ones(listed_group(g, 1))
            for c in range(columns // CHUNK):
                cols = pl.ds(c * CHUNK, CHUNK)
                scores = jnp.dot(k, qt_ref[:, cols], preferred_element_type=jnp.float32)
                if masked:
                    scores = jnp.where(allowed_group(g, CHUNK // BLOCK), scores, jnp.float32(-1e30))
                prob = jnp.exp2(scores * scale - m_ref[:1, cols] * scale).astype(jnp.bfloat16)
                acc_ref[(g + 1) % 2, :, cols] = acc_ref[g % 2, :, cols] + jnp.dot(
                    vt, prob, preferred_element_type=jnp.float32
                )

        def rescaled_update(g):
            k = listed_group(g, 0)
            vt = with_ones(listed_group(g, 1))
            for c in range(columns // CHUNK):
                cols = pl.ds(c * CHUNK, CHUNK)
                scores = jnp.dot(k, qt_ref[:, cols], preferred_element_type=jnp.float32)
                scores = jnp.where(allowed_group(g, CHUNK // BLOCK), scores, jnp.float32(-1e30))
                before = m_ref[:1, cols]
                newest = jnp.maximum(before, jnp.max(scores, axis=0, keepdims=True))
                prob = jnp.exp2(scores * scale - newest * scale).astype(jnp.bfloat16)
                rescale = jnp.exp2(before * scale - newest * scale)
                acc_ref[(g + 1) % 2, :, cols] = acc_ref[g % 2, :, cols] * rescale + jnp.dot(
                    vt, prob, preferred_element_type=jnp.float32
                )
                m_ref[:1, cols] = newest

        @pl.loop(0, groups)
        def _(g):
            masked = (g + 1) * GROUP > count
            for j in range(GROUP):
                masked = masked | (list_ref[b, g * GROUP + j] == first + b)

            @pl.when(masked)
            def _():
                update(g, True)

            @pl.when(jnp.logical_not(masked))
            def _():
                update(g, False)

            sums = acc_ref[(g + 1) % 2, HEAD_DIM : HEAD_DIM + 1]
            fits = jnp.min(jnp.where(sums < LARGEST, 1.0, 0.0)) > 0.5

            @pl.when(jnp.logical_not(fits))
            def _():
                rescaled_update(g)

        for head in range(per_kv):
            acc = acc_ref[groups % 2, :, head * BLOCK : (head + 1) * BLOCK]
            out = acc[:HEAD_DIM] / acc[HEAD_DIM : HEAD_DIM + 1]
            o_ref[query_rows, head_cols(head)] = out.T.astype(jnp.bfloat16)


def attend(entries, counts, queries, table):
    per_kv = queries.shape[1] // HEAD_DIM
    whole = pl.BlockSpec(memory_space=pltpu.VMEM)
    scalars = pl.BlockSpec(memory_space=pltpu.SMEM)
    return pl.pallas_call(
        attend_kernel,
        out_shape=jax.ShapeDtypeStruct(queries.shape, jnp.bfloat16),
        in_specs=[scalars, scalars, whole, whole],
        out_specs=whole,
        scratch_shapes=[
            pltpu.VMEM((HEAD_DIM, per_kv * BLOCK), jnp.bfloat16),
            pltpu.VMEM((8, per_kv * BLOCK), jnp.float32),
            pltpu.VMEM((2, HEAD_DIM + 16, per_kv * BLOCK), jnp.float32),
        ],
        compiler_params=pltpu.CompilerParams(vmem_limit_bytes=30 * 1024 * 1024),
    )(entries, counts, queries, table)


def return_kernel(heads, o_ref, out_ref, send, recv, local):
    rows = out_ref.shape[0]
    cols = o_ref.shape[1]
    s = lax.axis_index("seq")
    h = lax.axis_index("head")
    barrier = pltpu.get_barrier_semaphore()
    for _, peer in peers_of(h, heads):
        pl.semaphore_signal(barrier, inc=1, device_id=(s, peer), device_id_type=MESH)
    pl.semaphore_wait(barrier, heads - 1)
    mine = pl.ds(pl.multiple_of(h * cols, HEAD_DIM), cols)
    copies = []
    for d, peer in peers_of(h, heads):
        copies.append(
            pltpu.make_async_remote_copy(
                src_ref=o_ref.at[pl.ds(pl.multiple_of(peer * rows, 16), rows)],
                dst_ref=out_ref.at[:, mine],
                send_sem=send.at[d],
                recv_sem=recv.at[d],
                device_id=(s, peer),
                device_id_type=MESH,
            )
        )
    own = pltpu.make_async_copy(
        o_ref.at[pl.ds(pl.multiple_of(h * rows, 16), rows)], out_ref.at[:, mine], local
    )
    for copy in copies + [own]:
        copy.start()
    for copy in copies + [own]:
        copy.wait()


def give_back(attended, heads):
    rows, cols = attended.shape
    anywhere = pl.BlockSpec(memory_space=pl.ANY)
    return pl.pallas_call(
        functools.partial(return_kernel, heads),
        out_shape=jax.ShapeDtypeStruct((rows // heads, cols * heads), jnp.bfloat16),
        in_specs=[anywhere],
        out_specs=anywhere,
        scratch_shapes=[
            pltpu.SemaphoreType.DMA((heads,)),
            pltpu.SemaphoreType.DMA((heads,)),
            pltpu.SemaphoreType.DMA,
        ],
        compiler_params=pltpu.CompilerParams(collective_id=1, has_side_effects=True, vmem_limit_bytes=1024 * 1024),
    )(attended)


def per_device(queries, keys, values, block_list, block_count):
    shards = lax.axis_size("seq")
    heads = lax.axis_size("head")
    blocks = block_list.shape[1] // shards
    s = lax.axis_index("seq")
    h = lax.axis_index("head")
    width = block_list.shape[2]
    entries = lax.dynamic_slice(block_list, (h, s * blocks, 0), (1, blocks, width))[0]
    counts = lax.dynamic_slice(block_count, (h, s * blocks), (1, blocks))[0]
    queries, keys, values = (
        pltpu.with_memory_space_constraint(array, pltpu.HBM) for array in (queries, keys, values)
    )
    query_local, table = gather(queries, keys, values, shards, heads)
    attended = attend(entries, counts, query_local, table)
    return give_back(attended, heads)


def solution(mesh):
    placed = (
        P(("seq", "head"), None),
        P(("seq", "head"), None),
        P(("seq", "head"), None),
        P(),
        P(),
    )
    return jax.shard_map(
        per_device, mesh=mesh, in_specs=placed, out_specs=P(("seq", "head"), None), check_vma=False
    )
```

```python
import functools
import math

import jax
import jax.numpy as jnp
from jax import lax
from jax.experimental import pallas as pl
from jax.experimental.pallas import tpu as pltpu
from jax.sharding import PartitionSpec as P

HEADS = 64
KV_HEADS = 8
HEAD_DIM = 128
BLOCK = 128
GROUP = 16
CHUNK = 1024
LARGEST = 2.0**40
EARLY_PART = (10, 24)
LAG = 2
CORES = 2
HALVES = 2
MESH = pl.DeviceIdType.MESH
STEPS = ((1, 2), (1, 1), (1, 3), (1, 0), (0, 2), (0, 1), (0, 3))
OWN, RING, EARLY, CROSS, MATE, MATE_EARLY, MATE_CROSS = range(7)


def peers_of(h, heads):
    half = heads // 2
    return [(d + 1, (h // half + x) % 2 * half + (h % half + y) % half) for d, (x, y) in enumerate(STEPS)]


def gather_kernel(
    shards, heads, q_ref, k_ref, v_ref, qo_ref, tab_ref, kv_send, kv_recv, q_send, q_recv, send, recv, local
):
    rows = k_ref.shape[0]
    per_shard = tab_ref.shape[2]
    q_cols = q_ref.shape[1] // heads
    depth = shards // (CORES * HALVES)
    far = depth // 2
    early_rows = per_shard * EARLY_PART[0] // EARLY_PART[1]
    s = lax.axis_index("seq")
    h = lax.axis_index("head")
    core = s % CORES
    z = (s // CORES) % depth
    half = s // (CORES * depth)

    def seq_at(half_at, z_at):
        return (half_at * depth + z_at) * CORES + core

    up = seq_at(half, (z + 1) % depth)
    down = seq_at(half, (z + depth - 1) % depth)
    mate = s + 1 - 2 * core
    across = seq_at(1 - half, z)
    here = pl.ds(pl.multiple_of(h * rows, 16), rows)

    barrier = pltpu.get_barrier_semaphore()
    for _, peer in peers_of(h, heads):
        pl.semaphore_signal(barrier, inc=1, device_id=(s, peer), device_id_type=MESH)
    for other in (up, down, mate, across):
        pl.semaphore_signal(barrier, inc=1, device_id=(other, h), device_id_type=MESH)
    pl.semaphore_wait(barrier, heads + 3)

    def remote(src, dst, send_sem, recv_sem, to):
        return pltpu.make_async_remote_copy(
            src_ref=src, dst_ref=dst, send_sem=send_sem, recv_sem=recv_sem, device_id=to, device_id_type=MESH
        )

    kv_copies, q_copies = [], []
    for d, peer in peers_of(h, heads):
        cols = pl.ds(pl.multiple_of(peer * HEAD_DIM, HEAD_DIM), HEAD_DIM)
        for i, ref in enumerate((k_ref, v_ref)):
            kv_copies.append(
                remote(ref.at[:, cols], tab_ref.at[s, i, here], kv_send.at[i, d], kv_recv.at[i, d], (s, peer))
            )
        wide = pl.ds(pl.multiple_of(peer * q_cols, HEAD_DIM), q_cols)
        q_copies.append(remote(q_ref.at[:, wide], qo_ref.at[here], q_send.at[d], q_recv.at[d], (s, peer)))
    cols = pl.ds(pl.multiple_of(h * HEAD_DIM, HEAD_DIM), HEAD_DIM)
    wide = pl.ds(pl.multiple_of(h * q_cols, HEAD_DIM), q_cols)
    kv_local = [
        pltpu.make_async_copy(ref.at[:, cols], tab_ref.at[s, i, here], local.at[i])
        for i, ref in enumerate((k_ref, v_ref))
    ]
    q_local = pltpu.make_async_copy(q_ref.at[:, wide], qo_ref.at[here], local.at[2])
    for copy in kv_copies + kv_local:
        copy.start()
    for copy in kv_local:
        copy.wait()
    for copy in kv_copies:
        copy.wait_recv()

    def flow(mine):
        sent = []

        def copy_of(kind, way, slot, hops, other=False):
            z_at = (z - hops + depth) % depth if way == 0 else (z + hops) % depth
            half_at = mine if kind in (RING, MATE) else 0
            at = (half_at * depth + z_at) * CORES + (1 - core if other else core)
            if kind in (EARLY, MATE_EARLY, OWN):
                span = pl.ds(0, early_rows)
            elif kind in (CROSS, MATE_CROSS):
                span = pl.ds(early_rows, per_shard - early_rows)
            else:
                span = pl.ds(0, per_shard)
            ref = tab_ref.at[at, way, span] if slot == far else tab_ref.at[at, :, span]
            to = {RING: (up, down)[way], EARLY: (up, down)[way], OWN: across, CROSS: across}.get(kind, mate)
            return remote(ref, ref, send.at[kind, way, slot], recv.at[kind, way, slot], (to, h))

        def needed(kind, way, hops):
            if hops == 0:
                return None
            if kind == MATE:
                return z >= hops if way == 0 else z + hops >= depth
            if kind == RING and mine == 1:
                return z >= hops if way == 0 else (z + hops) % depth < far
            return None

        def onward(way, hops):
            if mine == 0:
                return None
            return (z >= hops) & (z + 1 < depth) if way == 0 else (z + hops) % depth < far

        def guarded(when, act):
            if when is None:
                act()
            else:
                pl.when(when)(act)

        def go(kind, way, hops):
            copy = copy_of(kind, way, hops + 1 if kind in (RING, EARLY) else hops, hops)
            when = onward(way, hops) if kind == RING else needed(kind, way, hops)
            guarded(when, copy.start)
            sent.append((when, copy))

        def arrive(kind, way, slot):
            copy = copy_of(kind, way, slot, slot, kind in (MATE, MATE_EARLY, MATE_CROSS))
            guarded(needed(kind, way, slot), copy.wait_recv)

        stages = [(0, 0)] + [(t, way) for t in range(1, far + 1) for way in (0, 1)]
        for way in (0, 1):
            go(RING, way, 0)
        if mine == 0:
            go(OWN, 0, 0)
            go(CROSS, 0, 0)
        go(MATE, 0, 0)
        for copy in q_copies + [q_local]:
            copy.start()
        if mine == 1:
            arrive(OWN, 0, 0)
            for way in (0, 1):
                go(EARLY, way, 0)
            go(MATE_EARLY, 0, 0)
        pending = [(0, 0)]
        for t in range(1, far + 1):
            for way in (0, 1):
                arrive(RING, way, t)
                if t < far:
                    go(RING, way, t)
            if mine == 1:
                for way in (0, 1):
                    arrive(EARLY, way, t)
                    if t < far:
                        go(EARLY, way, t)
            for way in (0, 1):
                if mine == 0:
                    go(CROSS, way, t)
                go(MATE, way, t)
                if mine == 1:
                    go(MATE_EARLY, way, t)
            if mine == 1:
                while pending and pending[0][0] < t - LAG:
                    at_t, at_way = pending.pop(0)
                    arrive(CROSS, at_way, at_t)
                    go(MATE_CROSS, at_way, at_t)
                pending += [(t, 0), (t, 1)]
        if mine == 1:
            for at_t, at_way in pending:
                arrive(CROSS, at_way, at_t)
                go(MATE_CROSS, at_way, at_t)
        for t, way in stages:
            arrive(MATE, way, t)
            if mine == 1:
                arrive(MATE_EARLY, way, t)
                arrive(MATE_CROSS, way, t)
        for when, copy in sent:
            guarded(when, copy.wait_send)

    @pl.when(half == 0)
    def _():
        flow(0)

    @pl.when(half == 1)
    def _():
        flow(1)

    for copy in kv_copies:
        copy.wait_send()
    q_local.wait()
    for copy in q_copies:
        copy.wait()


def gather(queries, keys, values, shards, heads):
    rows = queries.shape[0]
    depth = shards // (CORES * HALVES)
    far = depth // 2
    in_hbm = pl.BlockSpec(memory_space=pltpu.HBM)
    dma = pltpu.SemaphoreType.DMA
    return pl.pallas_call(
        functools.partial(gather_kernel, shards, heads),
        out_shape=(
            jax.ShapeDtypeStruct((rows * heads, queries.shape[1] // heads), jnp.bfloat16),
            jax.ShapeDtypeStruct((shards, 2, rows * heads, HEAD_DIM), jnp.bfloat16),
        ),
        in_specs=[in_hbm] * 3,
        out_specs=(pl.BlockSpec(memory_space=pltpu.VMEM),) * 2,
        scratch_shapes=[
            dma((2, heads)),
            dma((2, heads)),
            dma((heads,)),
            dma((heads,)),
            dma((7, 2, far + 1)),
            dma((7, 2, far + 1)),
            dma((3,)),
        ],
        compiler_params=pltpu.CompilerParams(collective_id=0, has_side_effects=True, vmem_limit_bytes=24 * 1024 * 1024),
    )(queries, keys, values)


def attend_kernel(list_ref, count_ref, q_ref, tab_ref, o_ref, qt_ref, m_ref, acc_ref):
    blocks = q_ref.shape[0] // BLOCK
    per_kv = q_ref.shape[1] // HEAD_DIM
    columns = per_kv * BLOCK
    scale = math.log2(math.e) / math.sqrt(HEAD_DIM)
    first = lax.axis_index("seq") * blocks

    def head_cols(head):
        return pl.ds(head * HEAD_DIM, HEAD_DIM)

    @pl.loop(0, blocks)
    def _(b):
        query_rows = pl.ds(pl.multiple_of(b * BLOCK, BLOCK), BLOCK)
        count = count_ref[lax.axis_index("head"), first + b]
        groups = (count + GROUP - 1) // GROUP
        for head in range(per_kv):
            qt_ref[:, head * BLOCK : (head + 1) * BLOCK] = q_ref[query_rows, head_cols(head)].T

        def listed(at, i):
            entry = jnp.where(at < count, list_ref[b, at], first)
            rows = pl.ds(pl.multiple_of((entry % blocks) * BLOCK, BLOCK), BLOCK)
            return tab_ref[entry // blocks, i, rows]

        def listed_group(g, i):
            return jnp.concatenate([listed(g * GROUP + j, i) for j in range(GROUP)], axis=0)

        def allowed(at):
            row = lax.broadcasted_iota(jnp.int32, (BLOCK, BLOCK), 1)
            col = lax.broadcasted_iota(jnp.int32, (BLOCK, BLOCK), 0)
            limit = jnp.where(list_ref[b, at] == first + b, row, jnp.full_like(row, BLOCK))
            limit = jnp.where(at < count, limit, jnp.full_like(row, -1))
            return (limit >= col).astype(jnp.int32)

        def allowed_group(g, heads):
            parts = jnp.concatenate([allowed(g * GROUP + j) for j in range(GROUP)], axis=0)
            return jnp.concatenate([parts] * heads, axis=1) > 0

        def with_ones(v):
            return jnp.concatenate([v.T, jnp.ones((16, v.shape[0]), v.dtype)], axis=0)

        scores = jnp.dot(listed(0, 0), qt_ref[...], preferred_element_type=jnp.float32)
        start = jnp.concatenate([allowed(0)] * per_kv, axis=1) > 0
        scores = jnp.where(start, scores, jnp.float32(-1e30))
        m_ref[:1] = jnp.max(scores, axis=0, keepdims=True)
        acc_ref[0] = jnp.zeros(acc_ref.shape[1:], jnp.float32)

        def update(g, masked):
            k = listed_group(g, 0)
            vt = with_ones(listed_group(g, 1))
            for c in range(columns // CHUNK):
                cols = pl.ds(c * CHUNK, CHUNK)
                scores = jnp.dot(k, qt_ref[:, cols], preferred_element_type=jnp.float32)
                if masked:
                    scores = jnp.where(allowed_group(g, CHUNK // BLOCK), scores, jnp.float32(-1e30))
                prob = jnp.exp2(scores * scale - m_ref[:1, cols] * scale).astype(jnp.bfloat16)
                acc_ref[(g + 1) % 2, :, cols] = acc_ref[g % 2, :, cols] + jnp.dot(
                    vt, prob, preferred_element_type=jnp.float32
                )

        def rescaled_update(g):
            k = listed_group(g, 0)
            vt = with_ones(listed_group(g, 1))
            for c in range(columns // CHUNK):
                cols = pl.ds(c * CHUNK, CHUNK)
                scores = jnp.dot(k, qt_ref[:, cols], preferred_element_type=jnp.float32)
                scores = jnp.where(allowed_group(g, CHUNK // BLOCK), scores, jnp.float32(-1e30))
                before = m_ref[:1, cols]
                newest = jnp.maximum(before, jnp.max(scores, axis=0, keepdims=True))
                prob = jnp.exp2(scores * scale - newest * scale).astype(jnp.bfloat16)
                rescale = jnp.exp2(before * scale - newest * scale)
                acc_ref[(g + 1) % 2, :, cols] = acc_ref[g % 2, :, cols] * rescale + jnp.dot(
                    vt, prob, preferred_element_type=jnp.float32
                )
                m_ref[:1, cols] = newest

        @pl.loop(0, groups)
        def _(g):
            masked = (g + 1) * GROUP > count
            for j in range(GROUP):
                masked = masked | (list_ref[b, g * GROUP + j] == first + b)

            @pl.when(masked)
            def _():
                update(g, True)

            @pl.when(jnp.logical_not(masked))
            def _():
                update(g, False)

            sums = acc_ref[(g + 1) % 2, HEAD_DIM : HEAD_DIM + 1]
            fits = jnp.min(jnp.where(sums < LARGEST, 1.0, 0.0)) > 0.5

            @pl.when(jnp.logical_not(fits))
            def _():
                rescaled_update(g)

        for head in range(per_kv):
            acc = acc_ref[groups % 2, :, head * BLOCK : (head + 1) * BLOCK]
            out = acc[:HEAD_DIM] / acc[HEAD_DIM : HEAD_DIM + 1]
            o_ref[query_rows, head_cols(head)] = out.T.astype(jnp.bfloat16)


def attend(entries, counts, queries, table):
    per_kv = queries.shape[1] // HEAD_DIM
    whole = pl.BlockSpec(memory_space=pltpu.VMEM)
    scalars = pl.BlockSpec(memory_space=pltpu.SMEM)
    return pl.pallas_call(
        attend_kernel,
        out_shape=jax.ShapeDtypeStruct(queries.shape, jnp.bfloat16),
        in_specs=[scalars, scalars, whole, whole],
        out_specs=whole,
        scratch_shapes=[
            pltpu.VMEM((HEAD_DIM, per_kv * BLOCK), jnp.bfloat16),
            pltpu.VMEM((8, per_kv * BLOCK), jnp.float32),
            pltpu.VMEM((2, HEAD_DIM + 16, per_kv * BLOCK), jnp.float32),
        ],
        compiler_params=pltpu.CompilerParams(vmem_limit_bytes=30 * 1024 * 1024),
    )(entries, counts, queries, table)


def return_kernel(heads, o_ref, out_ref, send, recv, local):
    rows = out_ref.shape[0]
    cols = o_ref.shape[1]
    s = lax.axis_index("seq")
    h = lax.axis_index("head")
    barrier = pltpu.get_barrier_semaphore()
    for _, peer in peers_of(h, heads):
        pl.semaphore_signal(barrier, inc=1, device_id=(s, peer), device_id_type=MESH)
    pl.semaphore_wait(barrier, heads - 1)
    mine = pl.ds(pl.multiple_of(h * cols, HEAD_DIM), cols)
    copies = []
    for d, peer in peers_of(h, heads):
        copies.append(
            pltpu.make_async_remote_copy(
                src_ref=o_ref.at[pl.ds(pl.multiple_of(peer * rows, 16), rows)],
                dst_ref=out_ref.at[:, mine],
                send_sem=send.at[d],
                recv_sem=recv.at[d],
                device_id=(s, peer),
                device_id_type=MESH,
            )
        )
    own = pltpu.make_async_copy(
        o_ref.at[pl.ds(pl.multiple_of(h * rows, 16), rows)], out_ref.at[:, mine], local
    )
    for copy in copies + [own]:
        copy.start()
    for copy in copies + [own]:
        copy.wait()


def give_back(attended, heads):
    rows, cols = attended.shape
    anywhere = pl.BlockSpec(memory_space=pl.ANY)
    return pl.pallas_call(
        functools.partial(return_kernel, heads),
        out_shape=jax.ShapeDtypeStruct((rows // heads, cols * heads), jnp.bfloat16),
        in_specs=[anywhere],
        out_specs=anywhere,
        scratch_shapes=[
            pltpu.SemaphoreType.DMA((heads,)),
            pltpu.SemaphoreType.DMA((heads,)),
            pltpu.SemaphoreType.DMA,
        ],
        compiler_params=pltpu.CompilerParams(collective_id=1, has_side_effects=True, vmem_limit_bytes=1024 * 1024),
    )(attended)


def per_device(queries, keys, values, block_list, block_count):
    shards = lax.axis_size("seq")
    heads = lax.axis_size("head")
    blocks = block_list.shape[1] // shards
    s = lax.axis_index("seq")
    h = lax.axis_index("head")
    width = block_list.shape[2]
    entries = lax.dynamic_slice(block_list, (h, s * blocks, 0), (1, blocks, width))[0]
    queries, keys, values = (
        pltpu.with_memory_space_constraint(array, pltpu.HBM) for array in (queries, keys, values)
    )
    query_local, table = gather(queries, keys, values, shards, heads)
    attended = attend(entries, block_count, query_local, table)
    return give_back(attended, heads)


def solution(mesh):
    placed = (
        P(("seq", "head"), None),
        P(("seq", "head"), None),
        P(("seq", "head"), None),
        P(),
        P(),
    )
    return jax.shard_map(
        per_device, mesh=mesh, in_specs=placed, out_specs=P(("seq", "head"), None), check_vma=False
    )
```
